256 devices in a mesh: tm: 8 (over y_hi, x), lat: 32 (over y_lo, z, core).
Axes of the slice: x: 4, y: 4 (y_hi: 2, y_lo: 2; y = y_hi * 2 + y_lo), z: 8, core: 2. Of those that a mesh axis runs over, the one named last changes fastest.
Arguments:
- frames: bfloat16 [128, 2048, 4096], P('tm', 'lat'), may hold values from -6 to 6
- owner_map: int32 [512], replicated, may hold values from 0 to 511, as said below
Outputs:
- spectrum: float32 [2, 512, 8, 1024], P(None, 'lat', None, 'tm')
The draws below stay inside these ranges and needn't reach their ends.
Inputs may be any that keep to these rules, and one draw needn't show every extreme that they name: owner_map is a permutation of 0 to 511; entries 2 i and 2 i + 1 hold an order m and the order 512 - 1 - m.
All inputs are finite; a program needn't handle non-finite values.
Results may differ from the reference program's by a relative error of at most 0.0064.
Values may be sent and summed in bfloat16 or wider, within the bound.
A program may use at most 64 MiB of HBM per device.

```python
import math
from functools import partial
import jax
import jax.numpy as jnp
from jax import lax

NLON = 4096
NLAT = 2048
M = 512
L = 1024
F = 8
FRAMES = 128


def draw_owner_map(key, part):
    pair_ids = jax.random.permutation(jax.random.fold_in(key, 11), M // 2).astype(jnp.int32)
    flips = jax.random.randint(jax.random.fold_in(key, 12), (M // 2,), 0, 2).astype(jnp.int32)
    leading = jnp.where(flips == 1, M - 1 - pair_ids, pair_ids)
    partner = M - 1 - leading
    return jnp.stack([leading, partner], axis=1).reshape(M).astype(jnp.int32)


def steps_of(key, extent, shards, low, high):
    gain = 1.0
    for position, parts in shards:
        heights = jax.random.uniform(jax.random.fold_in(jax.random.fold_in(key, 6), position), (parts,), jnp.float32, low / len(shards), high / len(shards))
        gain = gain * jnp.repeat(jnp.exp(heights), extent[position] // parts).reshape((-1,) + (1,) * (len(extent) - 1 - position))
    return gain


def bell_draw(stream_key, shape, deviation, limit, split=(), kind=jnp.bfloat16):
    gain = steps_of(stream_key, shape, split, -0.22, 0.18) if split else 1.0
    entries = jax.random.normal(stream_key, shape, jnp.float32) * deviation * gain
    return jnp.minimum(jnp.maximum(entries, -limit), limit).astype(kind)


def setup_inputs(seed: int = 0) -> dict:
    keys = jax.random.split(jax.random.key(seed), 3)
    frames = bell_draw(keys[0], (FRAMES, NLAT, NLON), 1.0, 6.0, ((0, 8), (1, 32)))
    owner_map = draw_owner_map(jax.random.fold_in(keys[2], 71), 0)
    return dict(frames=frames, owner_map=owner_map)


def longitude_table(owner_map, nlon_count):
    columns = owner_map.astype(jnp.int32)
    points = jnp.arange(nlon_count, dtype=jnp.int32)
    phases = points[:, None] * columns[None, :] % nlon_count
    angles = phases.astype(jnp.float32) * (2.0 * math.pi / nlon_count)
    factor = math.sqrt(2.0 / nlon_count)
    cos_part = (jnp.cos(angles) * factor).astype(jnp.bfloat16)
    sin_part = (-jnp.sin(angles) * factor).astype(jnp.bfloat16)
    return jnp.concatenate([cos_part, sin_part], axis=1)

def order_setup(orders, nlat_count, order_count):
    order_val = orders.astype(jnp.float32)[:, None]
    steps_k = jnp.arange(1, order_count + 1, dtype=jnp.float32)[None, :]
    growth = lax.optimization_barrier(jnp.sum(jnp.where(steps_k <= order_val, jnp.log1p(0.5 / steps_k), 0.0), axis=1, keepdims=True))
    colatitude = (jnp.arange(nlat_count, dtype=jnp.float32) + 0.5) * (math.pi / nlat_count)
    cosine = jnp.cos(colatitude)
    sine_row = jnp.sin(colatitude)
    lognorm = 0.5 * math.log(0.5) + 0.5 * growth + order_val * jnp.log(sine_row)[None, :]
    weight = sine_row * (math.pi / nlat_count) * math.sqrt(nlat_count)
    safe_log = jnp.maximum(lognorm, -60.0)
    start_value = jnp.where(lognorm >= -60.0, jnp.exp(safe_log), 0.0)
    diagonal_start = start_value * weight[None, :]
    return (order_val, cosine, diagonal_start)

def legendre_step(order_val, cosine, diagonal_start, state, degree):
    previous_p, older_p = state
    level = degree.astype(jnp.float32)
    level_sq = level * level
    order_sq = order_val * order_val
    lower = level - 1.0
    rising_coef = jnp.sqrt(jnp.maximum(4.0 * level_sq - 1.0, 0.0) / jnp.maximum(level_sq - order_sq, 1.0))
    falling_coef = jnp.sqrt(jnp.maximum(lower * lower - order_sq, 0.0) / jnp.maximum(4.0 * lower * lower - 1.0, 1.0))
    rising = rising_coef * (cosine[None, :] * previous_p - falling_coef * older_p)
    current = jnp.where(level == order_val, diagonal_start, jnp.where(level > order_val, rising, 0.0))
    return ((current, previous_p), current.astype(jnp.bfloat16))

def time_table(total_frames, band_count, first_frame, frame_count):
    frames_at = first_frame + jnp.arange(frame_count, dtype=jnp.int32)
    frequency = total_frames // 8 + jnp.arange(band_count, dtype=jnp.int32)
    phases = frequency[:, None] * frames_at[None, :] % total_frames
    angles = phases.astype(jnp.float32) * (2.0 * math.pi / total_frames)
    factor = 1.0 / math.sqrt(total_frames)
    cos_part = jnp.cos(angles) * factor
    sin_part = jnp.sin(angles) * factor
    top_row = jnp.stack([cos_part, sin_part], axis=1)
    low_row = jnp.stack([-sin_part, cos_part], axis=1)
    return jnp.stack([top_row, low_row], axis=0).astype(jnp.bfloat16)

def spectrum_block(band_block, orders, nlat_count, degree_count, order_count):
    order_val, cosine, diagonal_start = order_setup(orders, nlat_count, order_count)
    zero_rows = jnp.zeros(diagonal_start.shape, jnp.float32)
    stepper = partial(legendre_step, order_val, cosine, diagonal_start)
    _, polynomials = lax.scan(stepper, (zero_rows, zero_rows), jnp.arange(degree_count, dtype=jnp.int32))
    return jnp.einsum('ekfr,lkr->ekfl', band_block.astype(jnp.float32), polynomials.astype(jnp.float32))

def reference(frames, owner_map):
    lon_weights = longitude_table(owner_map, NLON).astype(jnp.float32)
    weights = time_table(FRAMES, F, 0, FRAMES).astype(jnp.float32)
    weight_cols = jnp.moveaxis(weights, 3, 0)

    def one_frame(total, packed):
        image, weight_col = packed
        coef = jnp.dot(image.astype(jnp.float32), lon_weights, precision=lax.Precision.HIGHEST).astype(jnp.bfloat16)
        coef = lax.optimization_barrier(coef).astype(jnp.float32).reshape(NLAT, 2, M)
        return (total + jnp.einsum('efc,rck->ekfr', weight_col, coef, precision=lax.Precision.HIGHEST), None)
    start_total = jnp.zeros((2, M, F, NLAT), jnp.float32)
    band, _ = lax.scan(one_frame, start_total, (frames, weight_cols))
    band = band.astype(jnp.bfloat16)
    group_size = min(32, M)
    group_count = M // group_size
    grouped = jnp.moveaxis(band.reshape(2, group_count, group_size, F, NLAT), 1, 0)
    orders = owner_map.reshape(group_count, group_size)

    def one_group(packed):
        return spectrum_block(packed[0], packed[1], NLAT, L, M)
    spectra = lax.map(one_group, (grouped, orders))
    return jnp.moveaxis(spectra, 0, 1).reshape(2, M, F, L)
```

```python
from functools import partial
import math

import jax
import jax.numpy as jnp
from jax import lax
from jax.experimental import pallas as pl
from jax.experimental.pallas import tpu as pltpu
from jax.sharding import PartitionSpec as P
import ml_dtypes
import numpy as np

L = 1024
F = 8
BF16 = jnp.bfloat16
F32 = jnp.float32


def longitude_tables(nlon, orders):
    half = nlon // 2
    points = np.arange(half, dtype=np.int64)[:, None]
    factor = math.sqrt(2.0 / nlon)
    tables = []
    for parity in range(2):
        order = np.arange(parity, orders, 2, dtype=np.int64)[None, :]
        angles = (points * order % nlon) * (2.0 * math.pi / nlon)
        tables.append(np.concatenate([np.cos(angles) * factor, -np.sin(angles) * factor], axis=1))
    return np.stack(tables).astype(np.float32).astype(ml_dtypes.bfloat16)


def time_tables(parts, frames, rows):
    total = parts * frames
    times = np.arange(total, dtype=np.int64)[None, :]
    frequency = (total // 8 + np.arange(F, dtype=np.int64))[:, None]
    angles = (frequency * times % total) * (2.0 * math.pi / total)
    cos_part = np.cos(angles) / math.sqrt(total)
    sin_part = np.sin(angles) / math.sqrt(total)
    real = np.concatenate([cos_part, -sin_part], axis=0)
    imag = np.concatenate([sin_part, cos_part], axis=0)
    table = np.stack([real, imag]).reshape(2, 2 * F, parts, frames).transpose(2, 0, 1, 3)
    wide = table[:, :, :, None, :, None] * np.eye(rows)[None, None, None, :, None, :]
    wide = wide.reshape(parts, 2, 2 * F * rows, frames * rows)
    return wide.astype(np.float32).astype(ml_dtypes.bfloat16)


def band_kernel(part_ref, frames_ref, tab_ref, wk_ref, own_ref, out_ref, bc_ref, ot_ref, oh_ref):
    step = pl.program_id(0)
    frame_count, rows, nlon = frames_ref.shape
    half = nlon // 2
    orders = own_ref.shape[1]
    pairs = orders // 2
    image = frames_ref[...].reshape(frame_count * rows, nlon)
    first, second = image[:, :half], image[:, half:]
    for parity in range(2):
        folded = first + second if parity == 0 else first - second
        coef = jnp.dot(folded, tab_ref[parity], preferred_element_type=F32).astype(BF16)
        part = jnp.dot(wk_ref[0, 0], coef[:, :pairs], preferred_element_type=F32)
        part = part + jnp.dot(wk_ref[0, 1], coef[:, pairs:], preferred_element_type=F32)
        row = pl.multiple_of(step * rows, rows)
        bc_ref[:, pl.ds(row, rows), parity * pairs : (parity + 1) * pairs] = part.astype(
            BF16
        ).reshape(2 * F, rows, pairs)

    @pl.when(step == 0)
    def _():
        wide = jnp.broadcast_to(own_ref[...].astype(F32), (128, orders))
        for block in range(orders // 128):
            ot_ref[block * 128 : (block + 1) * 128, :] = wide[:, block * 128 : (block + 1) * 128].T
        lane = lax.broadcasted_iota(jnp.int32, (32, orders), 1)
        order = jnp.where(lane < pairs, 2 * lane, 2 * (lane - pairs) + 1).astype(F32)
        for slot in range(2):
            for peer in range(8):
                held = ot_ref[pl.ds(2 * peer + slot, 32, stride=16), :]
                held = jnp.concatenate([held] * (orders // 128), axis=1)
                at = (slot * 8 + peer) * 32
                oh_ref[at : at + 32, :] = jnp.where(held == order, 1.0, 0.0).astype(BF16)

    @pl.when(step == pl.num_programs(0) - 1)
    def _():
        lat_rows = bc_ref.shape[1]
        flat = bc_ref[...].reshape(2 * F * lat_rows, orders)
        moved = [
            lax.dot_general(
                oh_ref[slot * pairs : (slot + 1) * pairs, :],
                flat,
                (((1,), (1,)), ((), ())),
                preferred_element_type=F32,
            ).astype(BF16)
            for slot in range(2)
        ]
        for ef in range(2 * F):
            at = slice(ef * lat_rows, (ef + 1) * lat_rows)
            out_ref[:, ef * 128 : (ef + 1) * 128] = jnp.concatenate(
                [moved[0][:, at], moved[1][:, at]], axis=1
            )


def partial_band(frames, owner_map, parts):
    frame_count, lat_rows, nlon = frames.shape
    orders = owner_map.shape[0]
    rows = 16
    tab = jnp.asarray(longitude_tables(nlon, orders))
    wk = jnp.asarray(time_tables(parts, frame_count, rows))
    size = frame_count * rows
    part = lax.axis_index("tm").astype(jnp.int32).reshape(1)
    return pl.pallas_call(
        band_kernel,
        out_shape=jax.ShapeDtypeStruct((orders // 2, 2 * F * 128), BF16),
        grid_spec=pltpu.PrefetchScalarGridSpec(
            num_scalar_prefetch=1,
            grid=(lat_rows // rows,),
            in_specs=[
                pl.BlockSpec((frame_count, rows, nlon), lambda i, part: (0, i, 0)),
                pl.BlockSpec((2, nlon // 2, orders), lambda i, part: (0, 0, 0), pipeline_mode=pl.Buffered(1)),
                pl.BlockSpec((1, 2, size, size), lambda i, part: (part[0], 0, 0, 0), pipeline_mode=pl.Buffered(1)),
                pl.BlockSpec((1, orders), lambda i, part: (0, 0)),
            ],
            out_specs=pl.BlockSpec((orders // 2, 2 * F * 128), lambda i, part: (0, 0)),
            scratch_shapes=[
                pltpu.VMEM((2 * F, lat_rows, orders), BF16),
                pltpu.VMEM((orders, 128), F32),
                pltpu.VMEM((orders, orders), BF16),
            ],
        ),
        compiler_params=pltpu.CompilerParams(
            dimension_semantics=("arbitrary",), vmem_limit_bytes=48 << 20
        ),
        name="partial_band",
    )(part, frames, tab, wk, owner_map.reshape(1, orders))


def latitude_constants(nlat, lat_rows):
    colatitude = (np.arange(nlat) + 0.5) * (math.pi / nlat)
    sine = np.sin(colatitude)
    weight = sine * (math.pi / nlat) * math.sqrt(nlat)

    def lay(values):
        values = values.reshape(nlat // lat_rows, lat_rows)
        return np.concatenate([values, values], axis=1)

    steps = np.log1p(0.5 / np.arange(1, 1025)).reshape(8, 128)
    grids = np.stack([lay(np.cos(colatitude)), lay(np.log(sine)), lay(weight)])
    return grids.astype(np.float32), steps.astype(np.float32)


def degree_factors(order, rise_ref, fall_ref):
    block = 64

    def body(i, carry):
        at = pl.multiple_of(i * block, block)
        level = (at + lax.broadcasted_iota(jnp.int32, (block, 128), 0)).astype(F32)
        level_sq = level * level
        order_sq = order * order
        lower = level - 1.0
        rising = jnp.sqrt(
            jnp.maximum(4.0 * level_sq - 1.0, 0.0) / jnp.maximum(level_sq - order_sq, 1.0)
        )
        falling = jnp.sqrt(
            jnp.maximum(lower * lower - order_sq, 0.0)
            / jnp.maximum(4.0 * lower * lower - 1.0, 1.0)
        )
        rise_ref[pl.ds(at, block), :] = rising
        fall_ref[pl.ds(at, block), :] = rising * falling
        return carry

    lax.fori_loop(0, L // block, body, 0)


def diagonal(order, grids_ref, steps_ref, held):
    step = (
        128 * lax.broadcasted_iota(jnp.int32, (8, 128), 0)
        + lax.broadcasted_iota(jnp.int32, (8, 128), 1)
        + 1
    )
    sums = [
        jnp.sum(jnp.where(step <= m, steps_ref[...], 0.0), axis=(0, 1), keepdims=True) for m in held
    ]
    lane = lax.broadcasted_iota(jnp.int32, (1, 128), 1)
    growth = jnp.where(lane < 64, sums[0], sums[1])
    lognorm = 0.5 * math.log(0.5) + 0.5 * growth + order * grids_ref[1]
    start = jnp.where(lognorm >= -60.0, jnp.exp(jnp.maximum(lognorm, -60.0)), 0.0)
    return start * grids_ref[2]


def fill_table(order, start, cosine, rise_ref, fall_ref, stage_ref, table_ref, lo, hi, state):
    groups = start.shape[0] // 8
    span = 16

    def body(i, carry):
        base = pl.multiple_of(i * span, span)
        newer, older = list(carry[0]), list(carry[1])
        for k in range(span):
            rise = jnp.broadcast_to(rise_ref[pl.ds(base + k, 1), :], (8, 128))
            fall = jnp.broadcast_to(fall_ref[pl.ds(base + k, 1), :], (8, 128))
            first = jnp.broadcast_to(order, (8, 128)) == (base + k).astype(F32)
            for g in range(groups):
                at = slice(8 * g, 8 * g + 8)
                now = (rise * cosine[at]) * newer[g] - fall * older[g]
                now = jnp.where(first, start[at], now)
                newer[g], older[g] = now, newer[g]
                stage_ref[(g * span + k) * 8 : (g * span + k) * 8 + 8, :] = now
        for g in range(groups):
            for j in range(8):
                rows = stage_ref[pl.ds(g * span * 8 + j, span, stride=8), :]
                table_ref[pl.ds(base, span), (8 * g + j) * 128 : (8 * g + j + 1) * 128] = (
                    rows.astype(BF16)
                )
        return tuple(newer), tuple(older)

    return lax.fori_loop(lo // span, hi // span, body, state)


def spectrum_kernel(first_ref, own_ref, band_ref, grids_ref, steps_ref, out_ref, rise_ref, fall_ref, stage_ref, table_ref, both_ref):
    m0 = own_ref[first_ref[0]]
    m1 = own_ref[first_ref[0] + 1]
    lane = lax.broadcasted_iota(jnp.int32, (1, 128), 1)
    order = jnp.where(lane < 64, m0, m1).astype(F32)
    degree_factors(order, rise_ref, fall_ref)
    start = diagonal(order, grids_ref, steps_ref, (m0, m1))
    cosine = grids_ref[0]
    count = start.shape[0]
    zeros = tuple(jnp.zeros((8, 128), F32) for _ in range(count // 8))
    fill_table(order, start, cosine, rise_ref, fall_ref, stage_ref, table_ref, 0, L, (zeros, zeros))
    lanes = lax.broadcasted_iota(jnp.int32, (16, 128), 1)
    for j in range(count):
        tile = band_ref[j]
        zero = jnp.zeros_like(tile)
        both_ref[0:16, j * 128 : (j + 1) * 128] = jnp.where(lanes < 64, tile, zero)
        both_ref[16:32, j * 128 : (j + 1) * 128] = jnp.where(lanes < 64, zero, tile)
    for q in range(L // 128):
        out_ref[q] = lax.dot_general(
            both_ref[...],
            table_ref[q * 128 : (q + 1) * 128, :],
            (((1,), (1,)), ((), ())),
            preferred_element_type=F32,
        )


def spectrum(band, owner_map, first_slot, nlat):
    groups = band.shape[0]
    grids, steps = latitude_constants(nlat, nlat // groups)
    vmem = pl.BlockSpec(memory_space=pltpu.VMEM)
    smem = pl.BlockSpec(memory_space=pltpu.SMEM)
    return pl.pallas_call(
        spectrum_kernel,
        out_shape=jax.ShapeDtypeStruct((L // 128, 4 * F, 128), F32),
        in_specs=[smem, smem, vmem, vmem, vmem],
        out_specs=vmem,
        scratch_shapes=[
            pltpu.VMEM((L, 128), F32),
            pltpu.VMEM((L, 128), F32),
            pltpu.VMEM((groups * 16, 128), F32),
            pltpu.VMEM((L, groups * 128), BF16),
            pltpu.VMEM((4 * F, groups * 128), BF16),
        ],
        compiler_params=pltpu.CompilerParams(vmem_limit_bytes=48 << 20),
        name="spectrum",
    )(first_slot.reshape(1), owner_map, band, jnp.asarray(grids), jnp.asarray(steps))


def shards(frames, owner_map):
    lat_count = lax.axis_size("lat")
    time_count = lax.axis_size("tm")
    orders = owner_map.shape[0]
    sent = partial_band(frames, owner_map, time_count)
    sent = sent.reshape(time_count, lat_count, 2 * F * 128)
    parts = lax.all_to_all(sent, "tm", split_axis=0, concat_axis=0, tiled=True)
    total = jnp.sum(parts.astype(F32), axis=0).astype(BF16).reshape(lat_count, 2 * F, 128)
    band = lax.all_to_all(total, "lat", split_axis=0, concat_axis=0, tiled=True)
    first_slot = lax.axis_index("lat") * (orders // lat_count) + lax.axis_index("tm") * 2
    pieces = spectrum(band, owner_map, first_slot.astype(jnp.int32), lat_count * frames.shape[1])
    pieces = lax.all_to_all(pieces, "tm", split_axis=0, concat_axis=0, tiled=True)
    pieces = pieces.reshape(time_count, 2, 2, F, 128).transpose(2, 0, 1, 3, 4)
    return pieces.reshape(2, 2 * time_count, F, 128)


def solution(mesh):
    return jax.shard_map(
        shards,
        mesh=mesh,
        in_specs=(P("tm", "lat", None), P()),
        out_specs=P(None, "lat", None, "tm"),
        check_vma=False,
    )
```

```python
from functools import partial
import math

import jax
import jax.numpy as jnp
from jax import lax
from jax.experimental import pallas as pl
from jax.experimental.pallas import tpu as pltpu
from jax.sharding import PartitionSpec as P
import numpy as np

L = 1024
F = 8
BF16 = jnp.bfloat16
MESH = pl.DeviceIdType.MESH
F32 = jnp.float32


def longitude_seeds(nlon, orders, fine):
    count = nlon // 2 // fine
    coarse, near = [], []
    for parity in range(2):
        order = np.arange(parity, orders, 2, dtype=np.int64)[None, :]
        for points, scale, out in (
            (np.arange(count, dtype=np.int64)[:, None] * fine, math.sqrt(2.0 / nlon), coarse),
            (np.arange(fine, dtype=np.int64)[:, None], 1.0, near),
        ):
            angles = (points * order % nlon) * (2.0 * math.pi / nlon)
            out.append(np.stack([np.cos(angles) * scale, np.sin(angles) * scale]))
    return np.stack(coarse).astype(np.float32), np.stack(near).astype(np.float32)


def time_tables(parts, frames, rows):
    total = parts * frames
    times = np.arange(total, dtype=np.int64)[None, :]
    frequency = (total // 8 + np.arange(F, dtype=np.int64))[:, None]
    angles = (frequency * times % total) * (2.0 * math.pi / total)
    cos_part = np.cos(angles) / math.sqrt(total)
    sin_part = np.sin(angles) / math.sqrt(total)
    real = np.concatenate([cos_part, -sin_part], axis=0)
    imag = np.concatenate([sin_part, cos_part], axis=0)
    table = np.stack([real, imag]).reshape(2, 2 * F, parts, frames).transpose(2, 0, 1, 3)
    return np.repeat(table, rows, axis=3).astype(np.float32)


def band_kernel(
    part_ref, frames_ref, coarse_ref, near_ref, time_ref, own_ref, out_ref,
    tab_ref, wk_ref, bc_ref, ot_ref, oh_ref,
):
    step = pl.program_id(0)
    frame_count, rows, nlon = frames_ref.shape
    half = nlon // 2
    orders = own_ref.shape[1]
    pairs = orders // 2

    @pl.when(step == 0)
    def _():
        fine = near_ref.shape[2]
        for parity in range(2):

            def body(i, carry):
                cos_row = coarse_ref[parity, 0, pl.ds(i, 1), :]
                sin_row = coarse_ref[parity, 1, pl.ds(i, 1), :]
                near_cos, near_sin = near_ref[parity, 0], near_ref[parity, 1]
                at = pl.ds(pl.multiple_of(i * fine, fine), fine)
                tab_ref[parity, at, :pairs] = (cos_row * near_cos - sin_row * near_sin).astype(BF16)
                tab_ref[parity, at, pairs:] = (-sin_row * near_cos - cos_row * near_sin).astype(BF16)
                return carry

            lax.fori_loop(0, half // fine, body, 0)
        size = frame_count * rows
        same = lax.broadcasted_iota(jnp.int32, (rows, size), 0) == lax.rem(
            lax.broadcasted_iota(jnp.int32, (rows, size), 1), rows
        )
        for c in range(2):
            for ef in range(2 * F):
                line = jnp.broadcast_to(time_ref[0, c, ef : ef + 1, :], (rows, size))
                wk_ref[c, ef * rows : (ef + 1) * rows, :] = jnp.where(same, line, 0.0).astype(BF16)
        wide = jnp.broadcast_to(own_ref[...].astype(F32), (128, orders))
        for block in range(orders // 128):
            ot_ref[block * 128 : (block + 1) * 128, :] = wide[:, block * 128 : (block + 1) * 128].T
        lane = lax.broadcasted_iota(jnp.int32, (32, orders), 1)
        order = jnp.where(lane < pairs, 2 * lane, 2 * (lane - pairs) + 1).astype(F32)
        for slot in range(2):
            for peer in range(8):
                held = ot_ref[pl.ds(2 * peer + slot, 32, stride=16), :]
                held = jnp.concatenate([held] * (orders // 128), axis=1)
                at = (slot * 8 + peer) * 32
                oh_ref[at : at + 32, :] = jnp.where(held == order, 1.0, 0.0).astype(BF16)

    image = frames_ref[...].reshape(frame_count * rows, nlon)
    first, second = image[:, :half], image[:, half:]
    for parity in range(2):
        folded = first + second if parity == 0 else first - second
        coef = jnp.dot(folded, tab_ref[parity], preferred_element_type=F32).astype(BF16)
        part = jnp.dot(wk_ref[0], coef[:, :pairs], preferred_element_type=F32)
        part = part + jnp.dot(wk_ref[1], coef[:, pairs:], preferred_element_type=F32)
        row = pl.multiple_of(step * rows, rows)
        bc_ref[:, pl.ds(row, rows), parity * pairs : (parity + 1) * pairs] = part.astype(
            BF16
        ).reshape(2 * F, rows, pairs)

    @pl.when(step == pl.num_programs(0) - 1)
    def _():
        lat_rows = bc_ref.shape[1]
        flat = bc_ref[...].reshape(2 * F * lat_rows, orders)
        moved = [
            lax.dot_general(
                oh_ref[slot * pairs : (slot + 1) * pairs, :],
                flat,
                (((1,), (1,)), ((), ())),
                preferred_element_type=F32,
            ).astype(BF16)
            for slot in range(2)
        ]
        for ef in range(2 * F):
            at = slice(ef * lat_rows, (ef + 1) * lat_rows)
            out_ref[:, ef * 128 : (ef + 1) * 128] = jnp.concatenate(
                [moved[0][:, at], moved[1][:, at]], axis=1
            )


def partial_band(frames, owner_map, parts):
    frame_count, lat_rows, nlon = frames.shape
    orders = owner_map.shape[0]
    rows, fine = 16, 64
    coarse, near = longitude_seeds(nlon, orders, fine)
    table = time_tables(parts, frame_count, rows)
    size = frame_count * rows
    part = lax.axis_index("tm").astype(jnp.int32).reshape(1)
    once = pl.Buffered(1)
    return pl.pallas_call(
        band_kernel,
        out_shape=jax.ShapeDtypeStruct((orders // 2, 2 * F * 128), BF16),
        grid_spec=pltpu.PrefetchScalarGridSpec(
            num_scalar_prefetch=1,
            grid=(lat_rows // rows,),
            in_specs=[
                pl.BlockSpec((frame_count, rows, nlon), lambda i, part: (0, i, 0)),
                pl.BlockSpec(coarse.shape, lambda i, part: (0, 0, 0, 0), pipeline_mode=once),
                pl.BlockSpec(near.shape, lambda i, part: (0, 0, 0, 0), pipeline_mode=once),
                pl.BlockSpec((1,) + table.shape[1:], lambda i, part: (part[0], 0, 0, 0), pipeline_mode=once),
                pl.BlockSpec((1, orders), lambda i, part: (0, 0)),
            ],
            out_specs=pl.BlockSpec((orders // 2, 2 * F * 128), lambda i, part: (0, 0)),
            scratch_shapes=[
                pltpu.VMEM((2, nlon // 2, orders), BF16),
                pltpu.VMEM((2, size, size), BF16),
                pltpu.VMEM((2 * F, lat_rows, orders), BF16),
                pltpu.VMEM((orders, 128), F32),
                pltpu.VMEM((orders, orders), BF16),
            ],
        ),
        compiler_params=pltpu.CompilerParams(
            dimension_semantics=("arbitrary",), vmem_limit_bytes=48 << 20
        ),
        name="partial_band",
    )(part, frames, jnp.asarray(coarse), jnp.asarray(near), jnp.asarray(table), owner_map.reshape(1, orders))


def latitude_constants(nlat, lat_rows):
    colatitude = (np.arange(nlat) + 0.5) * (math.pi / nlat)
    sine = np.sin(colatitude)
    weight = sine * (math.pi / nlat) * math.sqrt(nlat)

    def lay(values):
        values = values.reshape(nlat // lat_rows, lat_rows)
        return np.concatenate([values, values], axis=1)

    steps = np.log1p(0.5 / np.arange(1, 1025)).reshape(8, 128)
    grids = np.stack([lay(np.cos(colatitude)), lay(np.log(sine)), lay(weight)])
    return grids.astype(np.float32), steps.astype(np.float32)


def degree_factors(order, rise_ref, fall_ref):
    block = 64

    def body(i, carry):
        at = pl.multiple_of(i * block, block)
        level = (at + lax.broadcasted_iota(jnp.int32, (block, 128), 0)).astype(F32)
        level_sq = level * level
        order_sq = order * order
        lower = level - 1.0
        rising = jnp.sqrt(
            jnp.maximum(4.0 * level_sq - 1.0, 0.0) / jnp.maximum(level_sq - order_sq, 1.0)
        )
        falling = jnp.sqrt(
            jnp.maximum(lower * lower - order_sq, 0.0)
            / jnp.maximum(4.0 * lower * lower - 1.0, 1.0)
        )
        rise_ref[pl.ds(at, block), :] = rising
        fall_ref[pl.ds(at, block), :] = rising * falling
        return carry

    lax.fori_loop(0, L // block, body, 0)


def diagonal(order, grids_ref, steps_ref, held):
    step = (
        128 * lax.broadcasted_iota(jnp.int32, (8, 128), 0)
        + lax.broadcasted_iota(jnp.int32, (8, 128), 1)
        + 1
    )
    sums = [
        jnp.sum(jnp.where(step <= m, steps_ref[...], 0.0), axis=(0, 1), keepdims=True) for m in held
    ]
    lane = lax.broadcasted_iota(jnp.int32, (1, 128), 1)
    growth = jnp.where(lane < 64, sums[0], sums[1])
    lognorm = 0.5 * math.log(0.5) + 0.5 * growth + order * grids_ref[1]
    start = jnp.where(lognorm >= -60.0, jnp.exp(jnp.maximum(lognorm, -60.0)), 0.0)
    return start * grids_ref[2]


def fill_table(order, start, cosine, rise_ref, fall_ref, stage_ref, table_ref, lo, hi, state):
    groups = start.shape[0] // 8
    span = 16

    def body(i, carry):
        base = pl.multiple_of(i * span, span)
        newer, older = list(carry[0]), list(carry[1])
        for k in range(span):
            rise = jnp.broadcast_to(rise_ref[pl.ds(base + k, 1), :], (8, 128))
            fall = jnp.broadcast_to(fall_ref[pl.ds(base + k, 1), :], (8, 128))
            first = jnp.broadcast_to(order, (8, 128)) == (base + k).astype(F32)
            for g in range(groups):
                at = slice(8 * g, 8 * g + 8)
                now = (rise * cosine[at]) * newer[g] - fall * older[g]
                now = jnp.where(first, start[at], now)
                newer[g], older[g] = now, newer[g]
                stage_ref[(g * span + k) * 8 : (g * span + k) * 8 + 8, :] = now
        for g in range(groups):
            for j in range(8):
                rows = stage_ref[pl.ds(g * span * 8 + j, span, stride=8), :]
                table_ref[pl.ds(base, span), (8 * g + j) * 128 : (8 * g + j + 1) * 128] = (
                    rows.astype(BF16)
                )
        return tuple(newer), tuple(older)

    return lax.fori_loop(lo // span, hi // span, body, state)


def exchange_kernel(
    own_ref, sent_ref, grids_ref, steps_ref, out_ref,
    rise_ref, fall_ref, stage_ref, table_ref, both_ref,
    parts_ref, sum_ref, away_ref, band_ref, gone_ref, degrees_ref,
    part_send, part_recv, lat_send, lat_recv, deg_send, deg_recv,
):
    tm, lat = lax.axis_index("tm"), lax.axis_index("lat")
    time_count, lat_count = parts_ref.shape[0], band_ref.shape[0]

    def time_peer(d):
        return lax.rem(tm + d, time_count)

    def lat_peer(d):
        return lax.rem(lat + d, lat_count)

    barrier = pltpu.get_barrier_semaphore()

    def greet_time(d, carry):
        pl.semaphore_signal(barrier, inc=1, device_id={"tm": time_peer(d)}, device_id_type=MESH)
        return carry

    def greet_lat(d, carry):
        pl.semaphore_signal(barrier, inc=1, device_id={"lat": lat_peer(d)}, device_id_type=MESH)
        return carry

    lax.fori_loop(1, time_count, greet_time, 0)
    lax.fori_loop(1, lat_count, greet_lat, 0)
    pl.semaphore_wait(barrier, time_count + lat_count - 2)

    def part_copy(d):
        return pltpu.make_async_remote_copy(
            src_ref=sent_ref.at[time_peer(d)], dst_ref=parts_ref.at[tm],
            send_sem=part_send.at[d], recv_sem=part_recv.at[tm],
            device_id={"tm": time_peer(d)}, device_id_type=MESH,
        )

    def part_arrival(d):
        peer = time_peer(d)
        return pltpu.make_async_remote_copy(
            src_ref=sent_ref.at[peer], dst_ref=parts_ref.at[peer],
            send_sem=part_send.at[d], recv_sem=part_recv.at[peer],
            device_id={"tm": peer}, device_id_type=MESH,
        )

    def band_copy(d):
        return pltpu.make_async_remote_copy(
            src_ref=away_ref.at[lat_peer(d)], dst_ref=band_ref.at[lat],
            send_sem=lat_send.at[d], recv_sem=lat_recv.at[lat],
            device_id={"lat": lat_peer(d)}, device_id_type=MESH,
        )

    def band_arrival(d):
        peer = lat_peer(d)
        return pltpu.make_async_remote_copy(
            src_ref=away_ref.at[peer], dst_ref=band_ref.at[peer],
            send_sem=lat_send.at[d], recv_sem=lat_recv.at[peer],
            device_id={"lat": peer}, device_id_type=MESH,
        )

    def degree_copy(d):
        return pltpu.make_async_remote_copy(
            src_ref=gone_ref.at[time_peer(d)], dst_ref=degrees_ref.at[tm],
            send_sem=deg_send.at[d], recv_sem=deg_recv.at[tm],
            device_id={"tm": time_peer(d)}, device_id_type=MESH,
        )

    def degree_arrival(d):
        peer = time_peer(d)
        return pltpu.make_async_remote_copy(
            src_ref=gone_ref.at[peer], dst_ref=degrees_ref.at[peer],
            send_sem=deg_send.at[d], recv_sem=deg_recv.at[peer],
            device_id={"tm": peer}, device_id_type=MESH,
        )

    def run(first, last, action):
        def body(d, carry):
            action(d)
            return carry

        lax.fori_loop(first, last, body, 0)

    run(1, time_count, lambda d: part_copy(d).start())

    slot = lat * (2 * time_count) + tm * 2
    m0, m1 = own_ref[slot], own_ref[slot + 1]
    lane = lax.broadcasted_iota(jnp.int32, (1, 128), 1)
    order = jnp.where(lane < 64, m0, m1).astype(F32)
    degree_factors(order, rise_ref, fall_ref)
    start = diagonal(order, grids_ref, steps_ref, (m0, m1))
    zeros = tuple(jnp.zeros((8, 128), F32) for _ in range(lat_count // 8))
    fill_table(
        order, start, grids_ref[0], rise_ref, fall_ref, stage_ref, table_ref, 0, L, (zeros, zeros)
    )

    run(1, time_count, lambda d: part_arrival(d).wait_recv())
    for ef in range(2 * F):
        at = slice(ef * 128, (ef + 1) * 128)
        total = sent_ref[tm, :, at].astype(F32)
        for d in range(1, time_count):
            total = total + parts_ref[time_peer(d), :, at].astype(F32)
        sum_ref[pl.ds(ef, lat_count, stride=2 * F), :] = total
    away_ref[...] = sum_ref[...].astype(BF16).reshape(away_ref.shape)
    run(1, lat_count, lambda d: band_copy(d).start())
    band_ref[lat] = away_ref[lat]
    run(1, lat_count, lambda d: band_arrival(d).wait_recv())

    lanes = lax.broadcasted_iota(jnp.int32, (2 * F, 128), 1)
    for j in range(lat_count):
        tile = band_ref[j]
        zero = jnp.zeros_like(tile)
        at = slice(j * 128, (j + 1) * 128)
        both_ref[0 : 2 * F, at] = jnp.where(lanes < 64, tile, zero)
        both_ref[2 * F : 4 * F, at] = jnp.where(lanes < 64, zero, tile)

    def piece(q):
        return lax.dot_general(
            both_ref[...],
            table_ref[pl.ds(pl.multiple_of(q * 128, 128), 128), :],
            (((1,), (1,)), ((), ())),
            preferred_element_type=F32,
        )

    def send_piece(d):
        gone_ref[time_peer(d)] = piece(time_peer(d))
        degree_copy(d).start()

    run(1, time_count, send_piece)
    degrees_ref[tm] = piece(tm)
    run(1, time_count, lambda d: degree_arrival(d).wait_recv())
    for peer in range(time_count):
        for slot in range(2):
            for e in range(2):
                out_ref[e, 2 * peer + slot] = degrees_ref[peer, (2 * slot + e) * F : (2 * slot + e + 1) * F, :]
    run(1, time_count, lambda d: part_copy(d).wait_send())
    run(1, lat_count, lambda d: band_copy(d).wait_send())
    run(1, time_count, lambda d: degree_copy(d).wait_send())


def exchange(sent, owner_map, nlat):
    time_count, lat_count, width = sent.shape
    grids, steps = latitude_constants(nlat, nlat // lat_count)
    vmem = pl.BlockSpec(memory_space=pltpu.VMEM)
    smem = pl.BlockSpec(memory_space=pltpu.SMEM)
    dma = pltpu.SemaphoreType.DMA
    return pl.pallas_call(
        exchange_kernel,
        out_shape=jax.ShapeDtypeStruct((2, 2 * time_count, F, L // time_count), F32),
        in_specs=[smem, vmem, vmem, vmem],
        out_specs=vmem,
        scratch_shapes=[
            pltpu.VMEM((L, 128), F32),
            pltpu.VMEM((L, 128), F32),
            pltpu.VMEM((lat_count * 16, 128), F32),
            pltpu.VMEM((L, lat_count * 128), BF16),
            pltpu.VMEM((4 * F, lat_count * 128), BF16),
            pltpu.VMEM((time_count, lat_count, width), BF16),
            pltpu.VMEM((lat_count * 2 * F, 128), F32),
            pltpu.VMEM((lat_count, 2 * F, 128), BF16),
            pltpu.VMEM((lat_count, 2 * F, 128), BF16),
            pltpu.VMEM((time_count, 4 * F, 128), F32),
            pltpu.VMEM((time_count, 4 * F, 128), F32),
            dma((time_count,)), dma((time_count,)),
            dma((lat_count,)), dma((lat_count,)),
            dma((time_count,)), dma((time_count,)),
        ],
        compiler_params=pltpu.CompilerParams(
            vmem_limit_bytes=40 << 20, collective_id=0, has_side_effects=True
        ),
        name="exchange",
    )(owner_map, sent, jnp.asarray(grids), jnp.asarray(steps))


def shards(frames, owner_map):
    lat_count = lax.axis_size("lat")
    time_count = lax.axis_size("tm")
    sent = partial_band(frames, owner_map, time_count)
    sent = sent.reshape(time_count, lat_count, 2 * F * 128)
    return exchange(sent, owner_map, lat_count * frames.shape[1])


def solution(mesh):
    return jax.shard_map(
        shards,
        mesh=mesh,
        in_specs=(P("tm", "lat", None), P()),
        out_specs=P(None, "lat", None, "tm"),
        check_vma=False,
    )
```

```python
from functools import partial
import math

import jax
import jax.numpy as jnp
from jax import lax
from jax.experimental import pallas as pl
from jax.experimental.pallas import tpu as pltpu
from jax.sharding import PartitionSpec as P
import numpy as np

L = 1024
F = 8
BF16 = jnp.bfloat16
MESH = pl.DeviceIdType.MESH
F32 = jnp.float32


ROWS = 16
FINE = 64


def longitude_seeds(nlon, orders):
    count = nlon // 2 // FINE
    seeds = []
    for parity in range(2):
        order = np.arange(parity, orders, 2, dtype=np.int64)[None, :]
        points = np.concatenate([np.arange(count) * FINE, np.arange(FINE)])[:, None]
        angles = (points * order % nlon) * (2.0 * math.pi / nlon)
        scale = np.where(np.arange(count + FINE)[:, None] < count, math.sqrt(2.0 / nlon), 1.0)
        seeds.append(np.stack([np.cos(angles) * scale, np.sin(angles) * scale]))
    return np.stack(seeds).astype(np.float32)


def time_tables(parts, frames):
    total = parts * frames
    times = np.arange(total, dtype=np.int64)[None, :]
    frequency = (total // 8 + np.arange(F, dtype=np.int64))[:, None]
    angles = (frequency * times % total) * (2.0 * math.pi / total)
    cos_part = np.cos(angles) / math.sqrt(total)
    sin_part = np.sin(angles) / math.sqrt(total)
    real = np.concatenate([cos_part, -sin_part], axis=0)
    imag = np.concatenate([sin_part, cos_part], axis=0)
    table = np.stack([real, imag]).reshape(2, 2 * F, parts, frames).transpose(2, 0, 1, 3)
    return np.repeat(table, ROWS, axis=3).astype(np.float32)


def latitude_constants(nlat, lat_rows):
    colatitude = (np.arange(nlat // 2) + 0.5) * (math.pi / nlat)
    sine = np.sin(colatitude)
    weight = sine * (math.pi / nlat) * math.sqrt(nlat)

    def lay(values):
        values = values.reshape(-1, lat_rows // ROWS, 1, ROWS)
        return np.repeat(values, 2, axis=2).reshape(-1, 2 * lat_rows)

    steps = np.log1p(0.5 / np.arange(1, 1025)).reshape(8, 128)
    parts = [lay(np.cos(colatitude)), lay(np.log(sine)), lay(weight), steps]
    return np.concatenate(parts).astype(np.float32)


def longitude_table(seed_ref, tab_ref):
    pairs = seed_ref.shape[3]
    count = seed_ref.shape[2] - FINE
    for parity in range(2):

        def body(i, carry):
            cos_row = seed_ref[parity, 0, pl.ds(i, 1), :]
            sin_row = seed_ref[parity, 1, pl.ds(i, 1), :]
            near_cos, near_sin = seed_ref[parity, 0, count:], seed_ref[parity, 1, count:]
            at = pl.ds(pl.multiple_of(i * FINE, FINE), FINE)
            tab_ref[parity, at, :pairs] = (cos_row * near_cos - sin_row * near_sin).astype(BF16)
            tab_ref[parity, at, pairs:] = (-sin_row * near_cos - cos_row * near_sin).astype(BF16)
            return carry

        lax.fori_loop(0, count, body, 0)


def time_product_table(time_ref, wk_ref, flip):
    size = wk_ref.shape[1]
    row = lax.broadcasted_iota(jnp.int32, (ROWS, size), 0)
    lane = lax.rem(lax.broadcasted_iota(jnp.int32, (ROWS, size), 1), ROWS)
    same = row == jnp.where(flip, ROWS - 1 - lane, lane)
    for c in range(2):
        for ef in range(2 * F):
            line = jnp.broadcast_to(time_ref[c, ef : ef + 1, :], (ROWS, size))
            wk_ref[c, ef * ROWS : (ef + 1) * ROWS, :] = jnp.where(same, line, 0.0).astype(BF16)


def slot_table(own_ref, ot_ref, oh_ref, time_count, lat_count):
    orders = own_ref.shape[1]
    pairs = orders // 2
    wide = jnp.broadcast_to(own_ref[...].astype(F32), (128, orders))
    for block in range(orders // 128):
        ot_ref[block * 128 : (block + 1) * 128, :] = wide[:, block * 128 : (block + 1) * 128].T
    lane = lax.broadcasted_iota(jnp.int32, (lat_count, orders), 1)
    order = jnp.where(lane < pairs, 2 * lane, 2 * (lane - pairs) + 1).astype(F32)
    for slot in range(2):
        for peer in range(time_count):
            held = ot_ref[pl.ds(2 * peer + slot, lat_count, stride=2 * time_count), :]
            held = jnp.concatenate([held] * (orders // 128), axis=1)
            at = (slot * time_count + peer) * lat_count
            oh_ref[at : at + lat_count, :] = jnp.where(held == order, 1.0, 0.0).astype(BF16)


def degree_factors(order, rise_ref, fall_ref):
    block = 64

    def body(i, carry):
        at = pl.multiple_of(i * block, block)
        level = (at + lax.broadcasted_iota(jnp.int32, (block, 128), 0)).astype(F32)
        level_sq = level * level
        order_sq = order * order
        lower = level - 1.0
        rising = jnp.sqrt(
            jnp.maximum(4.0 * level_sq - 1.0, 0.0) / jnp.maximum(level_sq - order_sq, 1.0)
        )
        falling = jnp.sqrt(
            jnp.maximum(lower * lower - order_sq, 0.0)
            / jnp.maximum(4.0 * lower * lower - 1.0, 1.0)
        )
        rise_ref[pl.ds(at, block), :] = rising
        fall_ref[pl.ds(at, block), :] = rising * falling
        return carry

    lax.fori_loop(0, L // block, body, 0)


def diagonal(order, held, first, log_sine, weight, steps):
    step = (
        128 * lax.broadcasted_iota(jnp.int32, (8, 128), 0)
        + lax.broadcasted_iota(jnp.int32, (8, 128), 1)
        + 1
    ).astype(F32)
    sums = [jnp.sum(jnp.where(step <= m, steps, 0.0), axis=(0, 1), keepdims=True) for m in held]
    growth = jnp.where(first, sums[0], sums[1])
    lognorm = 0.5 * math.log(0.5) + 0.5 * growth + order * log_sine
    start = jnp.where(lognorm >= -60.0, jnp.exp(jnp.maximum(lognorm, -60.0)), 0.0)
    return start * weight


def fill_table(order, start, cosine, rise_ref, fall_ref, stage_ref, table_ref):
    groups = start.shape[0] // 8
    span = 16
    wide_order = jnp.broadcast_to(order, (8, 128))

    def body(i, carry):
        base = pl.multiple_of(i * span, span)
        newer, older = list(carry[0]), list(carry[1])
        for k in range(span):
            rise = jnp.broadcast_to(rise_ref[pl.ds(base + k, 1), :], (8, 128))
            fall = jnp.broadcast_to(fall_ref[pl.ds(base + k, 1), :], (8, 128))
            first = wide_order == (base + k).astype(F32)
            for g in range(groups):
                at = slice(8 * g, 8 * g + 8)
                now = (rise * cosine[at]) * newer[g] - fall * older[g]
                now = jnp.where(first, start[at], now)
                newer[g], older[g] = now, newer[g]
                stage_ref[(g * span + k) * 8 : (g * span + k) * 8 + 8, :] = now
        for g in range(groups):
            for j in range(8):
                rows = stage_ref[pl.ds(g * span * 8 + j, span, stride=8), :]
                table_ref[pl.ds(base, span), (8 * g + j) * 128 : (8 * g + j + 1) * 128] = (
                    rows.astype(BF16)
                )
        return tuple(newer), tuple(older)

    zeros = tuple(jnp.zeros((8, 128), F32) for _ in range(groups))
    lax.fori_loop(0, L // span, body, (zeros, zeros))


def run(first, last, action):
    def body(d, carry):
        action(d)
        return carry

    lax.fori_loop(first, last, body, 0)


def kernel(
    frames_ref, own_hbm, seed_hbm, time_hbm, grid_hbm, out_ref,
    image_ref, own_ref, seed_ref, time_ref, grid_ref,
    tab_ref, wk_ref, ot_ref, oh_ref, sent_ref,
    rise_ref, fall_ref, stage_ref, table_ref, both_ref,
    parts_ref, total_ref, sum_ref, away_ref, band_ref, gone_ref, degrees_ref,
    image_sem, load_sem, part_send, part_recv, lat_send, lat_recv, deg_send, deg_recv,
):
    tm, lat = lax.axis_index("tm"), lax.axis_index("lat")
    blocks, time_count, lat_count, width = parts_ref.shape
    frame_count, _, nlon = image_ref.shape[1:]
    half = nlon // 2
    pairs = seed_ref.shape[3]
    south = lat >= lat_count // 2
    north_count = lat_count // 2

    def time_peer(d):
        return lax.rem(tm + d, time_count)

    def lat_peer(d):
        return lax.rem(lat + d, lat_count)

    loads = [
        pltpu.make_async_copy(own_hbm, own_ref, load_sem.at[0]),
        pltpu.make_async_copy(seed_hbm, seed_ref, load_sem.at[1]),
        pltpu.make_async_copy(time_hbm.at[tm], time_ref, load_sem.at[2]),
        pltpu.make_async_copy(grid_hbm, grid_ref, load_sem.at[3]),
    ]
    for load in loads:
        load.start()

    def image_copy(g):
        at = pl.multiple_of(jnp.where(south, blocks - 1 - g, g) * ROWS, ROWS)
        return pltpu.make_async_copy(
            frames_ref.at[:, pl.ds(at, ROWS), :], image_ref.at[g], image_sem.at[g]
        )

    for g in range(blocks):
        image_copy(g).start()

    barrier = pltpu.get_barrier_semaphore()

    def greet_time(d):
        pl.semaphore_signal(barrier, inc=1, device_id={"tm": time_peer(d)}, device_id_type=MESH)

    def greet_lat(d):
        pl.semaphore_signal(barrier, inc=1, device_id={"lat": lat_peer(d)}, device_id_type=MESH)

    run(1, time_count, greet_time)
    run(1, lat_count, greet_lat)

    def part_copy(g, d):
        peer = time_peer(d)
        return pltpu.make_async_remote_copy(
            src_ref=sent_ref.at[g, peer], dst_ref=parts_ref.at[g, tm],
            send_sem=part_send.at[g, d], recv_sem=part_recv.at[g, tm],
            device_id={"tm": peer}, device_id_type=MESH,
        )

    def part_arrival(g, d):
        peer = time_peer(d)
        return pltpu.make_async_remote_copy(
            src_ref=sent_ref.at[g, peer], dst_ref=parts_ref.at[g, peer],
            send_sem=part_send.at[g, d], recv_sem=part_recv.at[g, peer],
            device_id={"tm": peer}, device_id_type=MESH,
        )

    def band_copy(d):
        return pltpu.make_async_remote_copy(
            src_ref=away_ref.at[lat_peer(d)], dst_ref=band_ref.at[lat],
            send_sem=lat_send.at[d], recv_sem=lat_recv.at[lat],
            device_id={"lat": lat_peer(d)}, device_id_type=MESH,
        )

    def band_arrival(d):
        peer = lat_peer(d)
        return pltpu.make_async_remote_copy(
            src_ref=away_ref.at[peer], dst_ref=band_ref.at[peer],
            send_sem=lat_send.at[d], recv_sem=lat_recv.at[peer],
            device_id={"lat": peer}, device_id_type=MESH,
        )

    def degree_copy(peer):
        return pltpu.make_async_remote_copy(
            src_ref=gone_ref.at[peer], dst_ref=degrees_ref.at[tm],
            send_sem=deg_send.at[peer], recv_sem=deg_recv.at[tm],
            device_id={"tm": peer}, device_id_type=MESH,
        )

    def degree_arrival(d):
        peer = time_peer(d)
        return pltpu.make_async_remote_copy(
            src_ref=gone_ref.at[peer], dst_ref=degrees_ref.at[peer],
            send_sem=deg_send.at[peer], recv_sem=deg_recv.at[peer],
            device_id={"tm": peer}, device_id_type=MESH,
        )

    for load in loads:
        load.wait()
    longitude_table(seed_ref, tab_ref)
    time_product_table(time_ref, wk_ref, south)
    slot_table(own_ref, ot_ref, oh_ref, time_count, lat_count)
    pl.semaphore_wait(barrier, time_count + lat_count - 2)

    def block(g):
        image_copy(g).wait()
        image = image_ref[g].reshape(frame_count * ROWS, nlon)
        first, second = image[:, :half], image[:, half:]
        bands = []
        for parity in range(2):
            folded = first + second if parity == 0 else first - second
            coef = jnp.dot(folded, tab_ref[parity], preferred_element_type=F32).astype(BF16)
            part = jnp.dot(wk_ref[0], coef[:, :pairs], preferred_element_type=F32)
            part = part + jnp.dot(wk_ref[1], coef[:, pairs:], preferred_element_type=F32)
            bands.append(part.astype(BF16))
        both = jnp.concatenate(bands, axis=1)
        moved = lax.dot_general(
            oh_ref[...], both, (((1,), (1,)), ((), ())), preferred_element_type=F32
        ).astype(BF16)
        for slot in range(2):
            sent_ref[g, :, :, slot * width // 2 : (slot + 1) * width // 2] = moved[
                slot * pairs : (slot + 1) * pairs
            ].reshape(time_count, lat_count, width // 2)
        run(1, time_count, lambda d: part_copy(g, d).start())

    run(0, blocks, block)

    slot = lat * (2 * time_count) + tm * 2
    held = [ot_ref[pl.ds(slot + s, 1), :] for s in range(2)]
    lane = lax.broadcasted_iota(jnp.int32, (1, 128), 1)
    first_slot = lax.rem(lane // ROWS, 2) == 0
    order = jnp.where(first_slot, held[0], held[1])
    degree_factors(order, rise_ref, fall_ref)
    cosine, log_sine, weight = (
        grid_ref[i * north_count : (i + 1) * north_count] for i in range(3)
    )
    steps = grid_ref[3 * north_count : 3 * north_count + 8]
    start = diagonal(order, held, first_slot, log_sine, weight, steps)
    fill_table(order, start, cosine, rise_ref, fall_ref, stage_ref, table_ref)

    def collect(g):
        run(1, time_count, lambda d: part_arrival(g, d).wait_recv())
        total = sent_ref[g, tm].astype(F32)
        for d in range(1, time_count):
            total = total + parts_ref[g, time_peer(d)].astype(F32)
        total_ref[g] = total

    run(0, blocks, collect)
    for ef in range(2 * F):
        pieces = [
            total_ref[g, :, s * width // 2 + ef * ROWS : s * width // 2 + (ef + 1) * ROWS]
            for g in range(blocks)
            for s in range(2)
        ]
        sum_ref[pl.ds(ef, lat_count, stride=2 * F), :] = jnp.concatenate(pieces, axis=1)
    away_ref[...] = sum_ref[...].astype(BF16).reshape(away_ref.shape)
    run(1, lat_count, lambda d: band_copy(d).start())
    band_ref[lat] = away_ref[lat]
    run(1, lat_count, lambda d: band_arrival(d).wait_recv())

    lanes = lax.broadcasted_iota(jnp.int32, (2 * F, 128), 1)
    mine = lax.rem(lanes // ROWS, 2) == 0
    for j in range(north_count):
        north = band_ref[j].astype(F32)
        mirror = band_ref[lat_count - 1 - j].astype(F32)
        at = slice(j * 128, (j + 1) * 128)
        for sign, tile in enumerate((north + mirror, north - mirror)):
            base = sign * 4 * F
            both_ref[base : base + 2 * F, at] = jnp.where(mine, tile, 0.0).astype(BF16)
            both_ref[base + 2 * F : base + 4 * F, at] = jnp.where(mine, 0.0, tile).astype(BF16)

    def product(d):
        pair = lax.rem(tm // 2 + d, time_count // 2)
        base = pl.multiple_of(pair * 256, 256)
        piece = lax.dot_general(
            both_ref[...],
            table_ref[pl.ds(base, 256), :],
            (((1,), (1,)), ((), ())),
            preferred_element_type=F32,
        )
        level = (base + lax.broadcasted_iota(jnp.int32, (2 * F, 256), 1)).astype(F32)
        for s in range(2):
            offset = level + held[s][:, :1]
            odd = offset - 2.0 * jnp.floor(offset * 0.5)
            at = slice(2 * F * s, 2 * F * (s + 1))
            even_part, odd_part = piece[at], piece[4 * F + 2 * F * s : 4 * F + 2 * F * (s + 1)]
            chosen = jnp.where(odd == 0.0, even_part, odd_part)
            for k in range(2):
                gone_ref[2 * pair + k, at] = chosen[:, k * 128 : (k + 1) * 128]
        for k in range(2):
            peer = 2 * pair + k

            @pl.when(peer != tm)
            def _():
                degree_copy(peer).start()

    run(1, time_count // 2 + 1, product)
    degrees_ref[tm] = gone_ref[tm]
    run(1, time_count, lambda d: degree_arrival(d).wait_recv())
    for peer in range(time_count):
        for s in range(2):
            for e in range(2):
                at = (2 * s + e) * F
                out_ref[e, 2 * peer + s] = degrees_ref[peer, at : at + F, :]
    run(0, blocks, lambda g: run(1, time_count, lambda d: part_copy(g, d).wait_send()))
    run(1, lat_count, lambda d: band_copy(d).wait_send())
    run(1, time_count, lambda d: degree_copy(time_peer(d)).wait_send())


def shards(frames, owner_map):
    lat_count = lax.axis_size("lat")
    time_count = lax.axis_size("tm")
    frame_count, lat_rows, nlon = frames.shape
    orders = owner_map.shape[0]
    blocks = lat_rows // ROWS
    size = frame_count * ROWS
    width = 2 * 2 * F * ROWS
    seeds = longitude_seeds(nlon, orders)
    times = time_tables(time_count, frame_count)
    grids = latitude_constants(lat_count * lat_rows, lat_rows)
    hbm = pl.BlockSpec(memory_space=pltpu.HBM)
    dma = pltpu.SemaphoreType.DMA
    return pl.pallas_call(
        kernel,
        out_shape=jax.ShapeDtypeStruct((2, 2 * time_count, F, L // time_count), F32),
        in_specs=[hbm] * 5,
        out_specs=pl.BlockSpec(memory_space=pltpu.VMEM),
        scratch_shapes=[
            pltpu.VMEM((blocks, frame_count, ROWS, nlon), BF16),
            pltpu.VMEM((1, orders), jnp.int32),
            pltpu.VMEM(seeds.shape, F32),
            pltpu.VMEM(times.shape[1:], F32),
            pltpu.VMEM(grids.shape, F32),
            pltpu.VMEM((2, nlon // 2, orders), BF16),
            pltpu.VMEM((2, size, size), BF16),
            pltpu.VMEM((orders, 128), F32),
            pltpu.VMEM((orders, orders), BF16),
            pltpu.VMEM((blocks, time_count, lat_count, width), BF16),
            pltpu.VMEM((L, 128), F32),
            pltpu.VMEM((L, 128), F32),
            pltpu.VMEM((lat_count * 8, 128), F32),
            pltpu.VMEM((L, lat_count * 64), BF16),
            pltpu.VMEM((8 * F, lat_count * 64), BF16),
            pltpu.VMEM((blocks, time_count, lat_count, width), BF16),
            pltpu.VMEM((blocks, lat_count, width), F32),
            pltpu.VMEM((lat_count * 2 * F, 128), F32),
            pltpu.VMEM((lat_count, 2 * F, 128), BF16),
            pltpu.VMEM((lat_count, 2 * F, 128), BF16),
            pltpu.VMEM((time_count, 4 * F, 128), F32),
            pltpu.VMEM((time_count, 4 * F, 128), F32),
            dma((blocks,)), dma((4,)),
            dma((blocks, time_count)), dma((blocks, time_count)),
            dma((lat_count,)), dma((lat_count,)),
            dma((time_count,)), dma((time_count,)),
        ],
        compiler_params=pltpu.CompilerParams(
            vmem_limit_bytes=56 << 20, collective_id=0, has_side_effects=True
        ),
        name="spectrum",
    )(
        frames, owner_map.reshape(1, orders),
        jnp.asarray(seeds), jnp.asarray(times), jnp.asarray(grids),
    )


def solution(mesh):
    return jax.shard_map(
        shards,
        mesh=mesh,
        in_specs=(P("tm", "lat", None), P()),
        out_specs=P(None, "lat", None, "tm"),
        check_vma=False,
    )
```

```python
from functools import partial
import math

import jax
import jax.numpy as jnp
from jax import lax
from jax.experimental import pallas as pl
from jax.experimental.pallas import tpu as pltpu
from jax.sharding import PartitionSpec as P
import numpy as np

L = 1024
F = 8
BF16 = jnp.bfloat16
MESH = pl.DeviceIdType.MESH
F32 = jnp.float32


ROWS = 16
FINE = 64


def longitude_seeds(nlon, orders):
    count = nlon // 2 // FINE
    seeds = []
    for parity in range(2):
        order = np.arange(parity, orders, 2, dtype=np.int64)[None, :]
        points = np.concatenate([np.arange(count) * FINE, np.arange(FINE)])[:, None]
        angles = (points * order % nlon) * (2.0 * math.pi / nlon)
        scale = np.where(np.arange(count + FINE)[:, None] < count, math.sqrt(2.0 / nlon), 1.0)
        seeds.append(np.stack([np.cos(angles) * scale, np.sin(angles) * scale]))
    return np.stack(seeds).astype(np.float32)


def time_tables(parts, frames):
    total = parts * frames
    times = np.arange(total, dtype=np.int64)[None, :]
    frequency = (total // 8 + np.arange(F, dtype=np.int64))[:, None]
    angles = (frequency * times % total) * (2.0 * math.pi / total)
    cos_part = np.cos(angles) / math.sqrt(total)
    sin_part = np.sin(angles) / math.sqrt(total)
    real = np.concatenate([cos_part, -sin_part], axis=0)
    imag = np.concatenate([sin_part, cos_part], axis=0)
    table = np.stack([real, imag]).reshape(2, 2 * F, parts, frames).transpose(2, 0, 1, 3)
    return np.repeat(table, ROWS, axis=3).astype(np.float32)


def latitude_constants(nlat, lat_rows):
    colatitude = (np.arange(nlat // 2) + 0.5) * (math.pi / nlat)
    sine = np.sin(colatitude)
    weight = sine * (math.pi / nlat) * math.sqrt(nlat)

    def lay(values):
        values = values.reshape(-1, 2, 2, lat_rows // ROWS // 2, 1, ROWS)
        values = np.repeat(values.transpose(2, 0, 1, 3, 4, 5), 2, axis=4)
        return values.reshape(-1, 2 * lat_rows)

    steps = np.log1p(0.5 / np.arange(1, 1025)).reshape(8, 128)
    parts = [lay(np.cos(colatitude)), lay(np.log(sine)), lay(weight), steps]
    return np.concatenate(parts).astype(np.float32)


def longitude_table(seed_ref, tab_ref):
    pairs = seed_ref.shape[3]
    count = seed_ref.shape[2] - FINE
    for parity in range(2):

        def body(i, carry):
            cos_row = seed_ref[parity, 0, pl.ds(i, 1), :]
            sin_row = seed_ref[parity, 1, pl.ds(i, 1), :]
            near_cos, near_sin = seed_ref[parity, 0, count:], seed_ref[parity, 1, count:]
            at = pl.ds(pl.multiple_of(i * FINE, FINE), FINE)
            tab_ref[parity, at, :pairs] = (cos_row * near_cos - sin_row * near_sin).astype(BF16)
            tab_ref[parity, at, pairs:] = (-sin_row * near_cos - cos_row * near_sin).astype(BF16)
            return carry

        lax.fori_loop(0, count, body, 0)


def time_product_table(time_ref, wk_ref, flip):
    size = wk_ref.shape[1]
    row = lax.broadcasted_iota(jnp.int32, (ROWS, size), 0)
    lane = lax.rem(lax.broadcasted_iota(jnp.int32, (ROWS, size), 1), ROWS)
    same = row == jnp.where(flip, ROWS - 1 - lane, lane)
    for c in range(2):
        for ef in range(2 * F):
            line = jnp.broadcast_to(time_ref[c, ef : ef + 1, :], (ROWS, size))
            wk_ref[c, ef * ROWS : (ef + 1) * ROWS, :] = jnp.where(same, line, 0.0).astype(BF16)


def slot_table(own_ref, ot_ref, oh_ref, time_count, lat_count):
    orders = own_ref.shape[1]
    pairs = orders // 2
    wide = jnp.broadcast_to(own_ref[...].astype(F32), (128, orders))
    for block in range(orders // 128):
        ot_ref[block * 128 : (block + 1) * 128, :] = wide[:, block * 128 : (block + 1) * 128].T
    lane = lax.broadcasted_iota(jnp.int32, (lat_count, orders), 1)
    order = jnp.where(lane < pairs, 2 * lane, 2 * (lane - pairs) + 1).astype(F32)
    for slot in range(2):
        for peer in range(time_count):
            held = ot_ref[pl.ds(2 * peer + slot, lat_count, stride=2 * time_count), :]
            held = jnp.concatenate([held] * (orders // 128), axis=1)
            at = (slot * time_count + peer) * lat_count
            oh_ref[at : at + lat_count, :] = jnp.where(held == order, 1.0, 0.0).astype(BF16)


def degree_factors(order, rise_ref, fall_ref):
    block = 64

    def body(i, carry):
        at = pl.multiple_of(i * block, block)
        level = (at + lax.broadcasted_iota(jnp.int32, (block, 128), 0)).astype(F32)
        level_sq = level * level
        order_sq = order * order
        lower = level - 1.0
        rising = jnp.sqrt(
            jnp.maximum(4.0 * level_sq - 1.0, 0.0) / jnp.maximum(level_sq - order_sq, 1.0)
        )
        falling = jnp.sqrt(
            jnp.maximum(lower * lower - order_sq, 0.0)
            / jnp.maximum(4.0 * lower * lower - 1.0, 1.0)
        )
        rise_ref[pl.ds(at, block), :] = rising
        fall_ref[pl.ds(at, block), :] = rising * falling
        return carry

    lax.fori_loop(0, L // block, body, 0)


def diagonal(order, held, first, log_sine, weight, steps):
    step = (
        128 * lax.broadcasted_iota(jnp.int32, (8, 128), 0)
        + lax.broadcasted_iota(jnp.int32, (8, 128), 1)
        + 1
    ).astype(F32)
    sums = [jnp.sum(jnp.where(step <= m, steps, 0.0), axis=(0, 1), keepdims=True) for m in held]
    growth = jnp.where(first, sums[0], sums[1])
    lognorm = 0.5 * math.log(0.5) + 0.5 * growth + order * log_sine
    start = jnp.where(lognorm >= -60.0, jnp.exp(jnp.maximum(lognorm, -60.0)), 0.0)
    return start * weight


def fill_table(order, start, cosine, rise_ref, fall_ref, stage_ref, table_ref):
    groups = start.shape[0] // 8
    span = 16
    wide_order = jnp.broadcast_to(order, (8, 128))

    def body(i, carry):
        base = pl.multiple_of(i * span, span)
        newer, older = list(carry[0]), list(carry[1])
        for k in range(span):
            rise = jnp.broadcast_to(rise_ref[pl.ds(base + k, 1), :], (8, 128))
            fall = jnp.broadcast_to(fall_ref[pl.ds(base + k, 1), :], (8, 128))
            first = wide_order == (base + k).astype(F32)
            for g in range(groups):
                at = slice(8 * g, 8 * g + 8)
                now = (rise * cosine[at]) * newer[g] - fall * older[g]
                now = jnp.where(first, start[at], now)
                newer[g], older[g] = now, newer[g]
                stage_ref[(g * span + k) * 8 : (g * span + k) * 8 + 8, :] = now
        for g in range(groups):
            for j in range(8):
                rows = stage_ref[pl.ds(g * span * 8 + j, span, stride=8), :]
                table_ref[pl.ds(base, span), (8 * g + j) * 128 : (8 * g + j + 1) * 128] = (
                    rows.astype(BF16)
                )
        return tuple(newer), tuple(older)

    zeros = tuple(jnp.zeros((8, 128), F32) for _ in range(groups))
    lax.fori_loop(0, L // span, body, (zeros, zeros))


def run(first, last, action):
    def body(d, carry):
        action(d)
        return carry

    if last - first < 8:
        for d in range(first, last):
            action(d)
    else:
        lax.fori_loop(first, last, body, 0)


def kernel(
    frames_ref, own_hbm, seed_hbm, time_hbm, grid_hbm, out_ref,
    image_ref, own_ref, seed_ref, time_ref, grid_ref,
    tab_ref, wk_ref, ot_ref, oh_ref, sent_ref,
    rise_ref, fall_ref, stage_ref, table_ref, both_ref, acc_ref,
    parts_ref, total_ref, sum_ref, away_ref, band_ref, gone_ref, degrees_ref,
    image_sem, load_sem, part_send, part_recv, lat_send, lat_recv, deg_send, deg_recv,
):
    tm, lat = lax.axis_index("tm"), lax.axis_index("lat")
    blocks, time_count, lat_count, width = parts_ref.shape
    frame_count, _, nlon = image_ref.shape[1:]
    half = nlon // 2
    pairs = seed_ref.shape[3]
    south = lat >= lat_count // 2
    north_count = lat_count // 2

    def wrap(value, count):
        return jnp.where(value >= count, value - count, value)

    def time_peer(d):
        return wrap(tm + d, time_count)

    def lat_peer(d):
        return wrap(lat + d, lat_count)

    loads = [
        pltpu.make_async_copy(own_hbm, own_ref, load_sem.at[0]),
        pltpu.make_async_copy(seed_hbm, seed_ref, load_sem.at[1]),
        pltpu.make_async_copy(time_hbm.at[tm], time_ref, load_sem.at[2]),
        pltpu.make_async_copy(grid_hbm, grid_ref, load_sem.at[3]),
    ]
    for load in loads:
        load.start()

    def image_copy(g):
        at = pl.multiple_of(jnp.where(south, blocks - 1 - g, g) * ROWS, ROWS)
        return pltpu.make_async_copy(
            frames_ref.at[:, pl.ds(at, ROWS), :], image_ref.at[g], image_sem.at[g]
        )

    for g in range(blocks):
        image_copy(g).start()

    barrier = pltpu.get_barrier_semaphore()

    def greet_time(d):
        pl.semaphore_signal(barrier, inc=1, device_id={"tm": time_peer(d)}, device_id_type=MESH)

    def greet_lat(d):
        pl.semaphore_signal(barrier, inc=1, device_id={"lat": lat_peer(d)}, device_id_type=MESH)

    run(1, time_count, greet_time)
    run(1, lat_count, greet_lat)

    def part_copy(g, d):
        peer = time_peer(d)
        return pltpu.make_async_remote_copy(
            src_ref=sent_ref.at[g, peer], dst_ref=parts_ref.at[g, tm],
            send_sem=part_send.at[g, d], recv_sem=part_recv.at[g, tm],
            device_id={"tm": peer}, device_id_type=MESH,
        )

    def part_arrival(g, d):
        peer = time_peer(d)
        return pltpu.make_async_remote_copy(
            src_ref=sent_ref.at[g, peer], dst_ref=parts_ref.at[g, peer],
            send_sem=part_send.at[g, d], recv_sem=part_recv.at[g, peer],
            device_id={"tm": peer}, device_id_type=MESH,
        )

    def band_copy(h, d):
        peer = lat_peer(d)
        return pltpu.make_async_remote_copy(
            src_ref=away_ref.at[h, peer], dst_ref=band_ref.at[h, lat],
            send_sem=lat_send.at[h, d], recv_sem=lat_recv.at[h, lat],
            device_id={"lat": peer}, device_id_type=MESH,
        )

    def band_arrival(h, d):
        peer = lat_peer(d)
        return pltpu.make_async_remote_copy(
            src_ref=away_ref.at[h, peer], dst_ref=band_ref.at[h, peer],
            send_sem=lat_send.at[h, d], recv_sem=lat_recv.at[h, peer],
            device_id={"lat": peer}, device_id_type=MESH,
        )

    def degree_copy(peer):
        return pltpu.make_async_remote_copy(
            src_ref=gone_ref.at[peer], dst_ref=degrees_ref.at[tm],
            send_sem=deg_send.at[peer], recv_sem=deg_recv.at[tm],
            device_id={"tm": peer}, device_id_type=MESH,
        )

    def degree_arrival(d):
        peer = time_peer(d)
        return pltpu.make_async_remote_copy(
            src_ref=gone_ref.at[peer], dst_ref=degrees_ref.at[peer],
            send_sem=deg_send.at[peer], recv_sem=deg_recv.at[peer],
            device_id={"tm": peer}, device_id_type=MESH,
        )

    for load in loads:
        load.wait()
    longitude_table(seed_ref, tab_ref)
    time_product_table(time_ref, wk_ref, south)
    slot_table(own_ref, ot_ref, oh_ref, time_count, lat_count)
    pl.semaphore_wait(barrier, time_count + lat_count - 2)

    def block(g):
        image_copy(g).wait()
        image = image_ref[g].reshape(frame_count * ROWS, nlon)
        first, second = image[:, :half], image[:, half:]
        bands = []
        for parity in range(2):
            folded = first + second if parity == 0 else first - second
            coef = jnp.dot(folded, tab_ref[parity], preferred_element_type=F32).astype(BF16)
            part = jnp.dot(wk_ref[0], coef[:, :pairs], preferred_element_type=F32)
            part = part + jnp.dot(wk_ref[1], coef[:, pairs:], preferred_element_type=F32)
            bands.append(part.astype(BF16))
        both = jnp.concatenate(bands, axis=1)
        moved = lax.dot_general(
            oh_ref[...], both, (((1,), (1,)), ((), ())), preferred_element_type=F32
        ).astype(BF16)
        for slot in range(2):
            sent_ref[g, :, :, slot * width // 2 : (slot + 1) * width // 2] = moved[
                slot * pairs : (slot + 1) * pairs
            ].reshape(time_count, lat_count, width // 2)
        run(1, time_count, lambda d: part_copy(g, d).start())

    lax.fori_loop(0, blocks, lambda g, carry: (block(g), carry)[1], 0)

    slot = lat * (2 * time_count) + tm * 2
    held = [ot_ref[pl.ds(slot + s, 1), :] for s in range(2)]
    lane = lax.broadcasted_iota(jnp.int32, (1, 128), 1)
    first_slot = lax.rem(lane // ROWS, 2) == 0
    order = jnp.where(first_slot, held[0], held[1])
    degree_factors(order, rise_ref, fall_ref)
    cosine, log_sine, weight = (
        grid_ref[i * north_count : (i + 1) * north_count] for i in range(3)
    )
    steps = grid_ref[3 * north_count : 3 * north_count + 8]
    start = diagonal(order, held, first_slot, log_sine, weight, steps)
    fill_table(order, start, cosine, rise_ref, fall_ref, stage_ref, table_ref)

    def collect(g):
        run(1, time_count, lambda d: part_arrival(g, d).wait_recv())
        total = sent_ref[g, tm].astype(F32)
        for d in range(1, time_count):
            total = total + parts_ref[g, time_peer(d)].astype(F32)
        total_ref[g] = total

    def send_half(h):
        held_blocks = range(h * blocks // 2, (h + 1) * blocks // 2)
        for g in held_blocks:
            collect(g)
        for low in range(F):
            pieces = [
                total_ref[g, :, base + ef * ROWS : base + (ef + 1) * ROWS]
                for ef in (low, low + F)
                for g in held_blocks
                for base in (0, width // 2)
            ]
            sum_ref[pl.ds(low, lat_count, stride=F), :] = jnp.concatenate(pieces, axis=1)
        away_ref[h] = sum_ref[...].astype(BF16).reshape(away_ref.shape[1:])
        run(1, lat_count, lambda d: band_copy(h, d).start())
        band_ref[h, lat] = away_ref[h, lat]

    for h in range(2):
        send_half(h)

    lanes = lax.broadcasted_iota(jnp.int32, (F, 128), 1)
    mine = lax.rem(lanes // ROWS, 2) == 0

    def receive_half(h):
        run(1, lat_count, lambda d: band_arrival(h, d).wait_recv())
        for pair in range(north_count // 2):
            north = [band_ref[h, 2 * pair + k].astype(F32) for k in range(2)]
            mirror = [band_ref[h, lat_count - 1 - 2 * pair - k].astype(F32) for k in range(2)]
            at = slice((h * north_count // 2 + pair) * 128, (h * north_count // 2 + pair + 1) * 128)
            for sign in range(2):
                tiles = [n - m if sign else n + m for n, m in zip(north, mirror)]
                parts = [
                    jnp.concatenate([tile[:, k * 64 : (k + 1) * 64] for tile in tiles], axis=1)
                    for k in range(2)
                ]
                whole = jnp.concatenate(parts, axis=0)
                both_mine = jnp.concatenate([mine, mine], axis=0)
                base = sign * 4 * F
                both_ref[base : base + 2 * F, at] = jnp.where(both_mine, whole, 0.0).astype(BF16)
                both_ref[base + 2 * F : base + 4 * F, at] = jnp.where(
                    both_mine, 0.0, whole
                ).astype(BF16)

    depth = both_ref.shape[1] // 2

    def half_product(h, base):
        return lax.dot_general(
            both_ref[:, h * depth : (h + 1) * depth],
            table_ref[pl.ds(base, 256), h * depth : (h + 1) * depth],
            (((1,), (1,)), ((), ())),
            preferred_element_type=F32,
        )

    receive_half(0)
    for base in range(0, L, 256):
        acc_ref[base // 256] = half_product(0, base)
    receive_half(1)

    def product(d):
        pair = wrap(tm // 2 + d, time_count // 2)
        base = pl.multiple_of(pair * 256, 256)
        piece = acc_ref[pair] + half_product(1, base)
        level = (base + lax.broadcasted_iota(jnp.int32, (2 * F, 256), 1)).astype(F32)
        for s in range(2):
            offset = level + held[s][:, :1]
            odd = offset - 2.0 * jnp.floor(offset * 0.5)
            at = slice(2 * F * s, 2 * F * (s + 1))
            even_part, odd_part = piece[at], piece[4 * F + 2 * F * s : 4 * F + 2 * F * (s + 1)]
            chosen = jnp.where(odd == 0.0, even_part, odd_part)
            for k in range(2):
                gone_ref[2 * pair + k, at] = chosen[:, k * 128 : (k + 1) * 128]
        for k in range(2):
            peer = 2 * pair + k

            @pl.when(peer != tm)
            def _():
                degree_copy(peer).start()

    for d in range(1, time_count // 2 + 1):
        product(d)
    degrees_ref[tm] = gone_ref[tm]
    run(1, time_count, lambda d: degree_arrival(d).wait_recv())
    for peer in range(time_count):
        for s in range(2):
            for e in range(2):
                at = (2 * s + e) * F
                out_ref[e, 2 * peer + s] = degrees_ref[peer, at : at + F, :]
    run(0, blocks, lambda g: run(1, time_count, lambda d: part_copy(g, d).wait_send()))
    for h in range(2):
        run(1, lat_count, lambda d: band_copy(h, d).wait_send())
    run(1, time_count, lambda d: degree_copy(time_peer(d)).wait_send())


def shards(frames, owner_map):
    lat_count = lax.axis_size("lat")
    time_count = lax.axis_size("tm")
    frame_count, lat_rows, nlon = frames.shape
    orders = owner_map.shape[0]
    blocks = lat_rows // ROWS
    size = frame_count * ROWS
    width = 2 * 2 * F * ROWS
    seeds = longitude_seeds(nlon, orders)
    times = time_tables(time_count, frame_count)
    grids = latitude_constants(lat_count * lat_rows, lat_rows)
    hbm = pl.BlockSpec(memory_space=pltpu.HBM)
    dma = pltpu.SemaphoreType.DMA
    return pl.pallas_call(
        kernel,
        out_shape=jax.ShapeDtypeStruct((2, 2 * time_count, F, L // time_count), F32),
        in_specs=[hbm] * 5,
        out_specs=pl.BlockSpec(memory_space=pltpu.VMEM),
        scratch_shapes=[
            pltpu.VMEM((blocks, frame_count, ROWS, nlon), BF16),
            pltpu.VMEM((1, orders), jnp.int32),
            pltpu.VMEM(seeds.shape, F32),
            pltpu.VMEM(times.shape[1:], F32),
            pltpu.VMEM(grids.shape, F32),
            pltpu.VMEM((2, nlon // 2, orders), BF16),
            pltpu.VMEM((2, size, size), BF16),
            pltpu.VMEM((orders, 128), F32),
            pltpu.VMEM((orders, orders), BF16),
            pltpu.VMEM((blocks, time_count, lat_count, width), BF16),
            pltpu.VMEM((L, 128), F32),
            pltpu.VMEM((L, 128), F32),
            pltpu.VMEM((lat_count * 8, 128), F32),
            pltpu.VMEM((L, lat_count * 64), BF16),
            pltpu.VMEM((8 * F, lat_count * 64), BF16),
            pltpu.VMEM((L // 256, 8 * F, 256), F32),
            pltpu.VMEM((blocks, time_count, lat_count, width), BF16),
            pltpu.VMEM((blocks, lat_count, width), F32),
            pltpu.VMEM((lat_count * F, 128), F32),
            pltpu.VMEM((2, lat_count, F, 128), BF16),
            pltpu.VMEM((2, lat_count, F, 128), BF16),
            pltpu.VMEM((time_count, 4 * F, 128), F32),
            pltpu.VMEM((time_count, 4 * F, 128), F32),
            dma((blocks,)), dma((4,)),
            dma((blocks, time_count)), dma((blocks, time_count)),
            dma((2, lat_count)), dma((2, lat_count)),
            dma((time_count,)), dma((time_count,)),
        ],
        compiler_params=pltpu.CompilerParams(
            vmem_limit_bytes=56 << 20, collective_id=0, has_side_effects=True
        ),
        name="spectrum",
    )(
        frames, owner_map.reshape(1, orders),
        jnp.asarray(seeds), jnp.asarray(times), jnp.asarray(grids),
    )


def solution(mesh):
    return jax.shard_map(
        shards,
        mesh=mesh,
        in_specs=(P("tm", "lat", None), P()),
        out_specs=P(None, "lat", None, "tm"),
        check_vma=False,
    )
```

```python
from functools import partial
import math

import jax
import jax.numpy as jnp
from jax import lax
from jax.experimental import pallas as pl
from jax.experimental.pallas import tpu as pltpu
from jax.sharding import PartitionSpec as P
import numpy as np

L = 1024
F = 8
BF16 = jnp.bfloat16
MESH = pl.DeviceIdType.MESH
F32 = jnp.float32


ROWS = 16
ORDER = ((2, 1), (1, 1), (3, 1), (0, 1), (2, 0), (1, 0), (3, 0))
FINE = 64


def longitude_seeds(nlon, orders):
    count = nlon // 2 // FINE
    seeds = []
    for parity in range(2):
        order = np.arange(parity, orders, 2, dtype=np.int64)[None, :]
        points = np.concatenate([np.arange(count) * FINE, np.arange(FINE)])[:, None]
        angles = (points * order % nlon) * (2.0 * math.pi / nlon)
        scale = np.where(np.arange(count + FINE)[:, None] < count, math.sqrt(2.0 / nlon), 1.0)
        seeds.append(np.stack([np.cos(angles) * scale, np.sin(angles) * scale]))
    return np.stack(seeds).astype(np.float32)


def time_tables(parts, frames):
    total = parts * frames
    times = np.arange(total, dtype=np.int64)[None, :]
    frequency = (total // 8 + np.arange(F, dtype=np.int64))[:, None]
    angles = (frequency * times % total) * (2.0 * math.pi / total)
    cos_part = np.cos(angles) / math.sqrt(total)
    sin_part = np.sin(angles) / math.sqrt(total)
    real = np.concatenate([cos_part, -sin_part], axis=0)
    imag = np.concatenate([sin_part, cos_part], axis=0)
    table = np.stack([real, imag]).reshape(2, 2 * F, parts, frames).transpose(2, 0, 1, 3)
    return np.repeat(table, ROWS, axis=3).astype(np.float32)


def latitude_constants(nlat, lat_rows):
    colatitude = (np.arange(nlat // 2) + 0.5) * (math.pi / nlat)
    sine = np.sin(colatitude)
    weight = sine * (math.pi / nlat) * math.sqrt(nlat)

    def lay(values):
        values = values.reshape(-1, 2, 2, lat_rows // ROWS // 2, 1, ROWS)
        values = np.repeat(values.transpose(2, 0, 1, 3, 4, 5), 2, axis=4)
        return values.reshape(-1, 2 * lat_rows)

    steps = np.log1p(0.5 / np.arange(1, 1025)).reshape(8, 128)
    parts = [lay(np.cos(colatitude)), lay(np.log(sine)), lay(weight), steps]
    return np.concatenate(parts).astype(np.float32)


def longitude_table(seed_ref, tab_ref):
    pairs = seed_ref.shape[3]
    count = seed_ref.shape[2] - FINE
    for parity in range(2):

        def body(i, carry):
            cos_row = seed_ref[parity, 0, pl.ds(i, 1), :]
            sin_row = seed_ref[parity, 1, pl.ds(i, 1), :]
            near_cos, near_sin = seed_ref[parity, 0, count:], seed_ref[parity, 1, count:]
            at = pl.ds(pl.multiple_of(i * FINE, FINE), FINE)
            tab_ref[parity, at, :pairs] = (cos_row * near_cos - sin_row * near_sin).astype(BF16)
            tab_ref[parity, at, pairs:] = (-sin_row * near_cos - cos_row * near_sin).astype(BF16)
            return carry

        lax.fori_loop(0, count, body, 0)


def time_product_table(time_ref, wk_ref, flip):
    size = wk_ref.shape[1]
    row = lax.broadcasted_iota(jnp.int32, (ROWS, size), 0)
    lane = lax.rem(lax.broadcasted_iota(jnp.int32, (ROWS, size), 1), ROWS)
    same = row == jnp.where(flip, ROWS - 1 - lane, lane)
    for c in range(2):
        for ef in range(2 * F):
            line = jnp.broadcast_to(time_ref[c, ef : ef + 1, :], (ROWS, size))
            wk_ref[c, ef * ROWS : (ef + 1) * ROWS, :] = jnp.where(same, line, 0.0).astype(BF16)


def slot_table(own_ref, ot_ref, oh_ref, time_count, lat_count):
    orders = own_ref.shape[1]
    pairs = orders // 2
    wide = jnp.broadcast_to(own_ref[...].astype(F32), (128, orders))
    for block in range(orders // 128):
        ot_ref[block * 128 : (block + 1) * 128, :] = wide[:, block * 128 : (block + 1) * 128].T
    lane = lax.broadcasted_iota(jnp.int32, (lat_count, orders), 1)
    order = jnp.where(lane < pairs, 2 * lane, 2 * (lane - pairs) + 1).astype(F32)
    for slot in range(2):
        for peer in range(time_count):
            held = ot_ref[pl.ds(2 * peer + slot, lat_count, stride=2 * time_count), :]
            held = jnp.concatenate([held] * (orders // 128), axis=1)
            at = (slot * time_count + peer) * lat_count
            oh_ref[at : at + lat_count, :] = jnp.where(held == order, 1.0, 0.0).astype(BF16)


def degree_factors(order, rise_ref, fall_ref):
    block = 64

    def body(i, carry):
        at = pl.multiple_of(i * block, block)
        level = (at + lax.broadcasted_iota(jnp.int32, (block, 128), 0)).astype(F32)
        level_sq = level * level
        order_sq = order * order
        lower = level - 1.0
        rising = jnp.sqrt(
            jnp.maximum(4.0 * level_sq - 1.0, 0.0) / jnp.maximum(level_sq - order_sq, 1.0)
        )
        falling = jnp.sqrt(
            jnp.maximum(lower * lower - order_sq, 0.0)
            / jnp.maximum(4.0 * lower * lower - 1.0, 1.0)
        )
        rise_ref[pl.ds(at, block), :] = rising
        fall_ref[pl.ds(at, block), :] = rising * falling
        return carry

    lax.fori_loop(0, L // block, body, 0)


def diagonal(order, held, first, log_sine, weight, steps):
    step = (
        128 * lax.broadcasted_iota(jnp.int32, (8, 128), 0)
        + lax.broadcasted_iota(jnp.int32, (8, 128), 1)
        + 1
    ).astype(F32)
    sums = [jnp.sum(jnp.where(step <= m, steps, 0.0), axis=(0, 1), keepdims=True) for m in held]
    growth = jnp.where(first, sums[0], sums[1])
    lognorm = 0.5 * math.log(0.5) + 0.5 * growth + order * log_sine
    start = jnp.where(lognorm >= -60.0, jnp.exp(jnp.maximum(lognorm, -60.0)), 0.0)
    return start * weight


def fill_table(order, start, cosine, rise_ref, fall_ref, stage_ref, table_ref):
    groups = start.shape[0] // 8
    span = 16
    wide_order = jnp.broadcast_to(order, (8, 128))

    def body(i, carry):
        base = pl.multiple_of(i * span, span)
        newer, older = list(carry[0]), list(carry[1])
        for k in range(span):
            rise = jnp.broadcast_to(rise_ref[pl.ds(base + k, 1), :], (8, 128))
            fall = jnp.broadcast_to(fall_ref[pl.ds(base + k, 1), :], (8, 128))
            first = wide_order == (base + k).astype(F32)
            for g in range(groups):
                at = slice(8 * g, 8 * g + 8)
                now = (rise * cosine[at]) * newer[g] - fall * older[g]
                now = jnp.where(first, start[at], now)
                newer[g], older[g] = now, newer[g]
                stage_ref[(g * span + k) * 8 : (g * span + k) * 8 + 8, :] = now
        for g in range(groups):
            for j in range(8):
                rows = stage_ref[pl.ds(g * span * 8 + j, span, stride=8), :]
                table_ref[pl.ds(base, span), (8 * g + j) * 128 : (8 * g + j + 1) * 128] = (
                    rows.astype(BF16)
                )
        return tuple(newer), tuple(older)

    zeros = tuple(jnp.zeros((8, 128), F32) for _ in range(groups))
    lax.fori_loop(0, L // span, body, (zeros, zeros))


def run(first, last, action):
    def body(d, carry):
        action(d)
        return carry

    if last - first < 8:
        for d in range(first, last):
            action(d)
    else:
        lax.fori_loop(first, last, body, 0, unroll=True)


def kernel(
    frames_ref, own_hbm, seed_hbm, time_hbm, grid_hbm, out_ref,
    image_ref, own_ref, seed_ref, time_ref, grid_ref,
    tab_ref, wk_ref, ot_ref, oh_ref, sent_ref,
    rise_ref, fall_ref, stage_ref, table_ref, both_ref, acc_ref,
    parts_ref, total_ref, sum_ref, away_ref, band_ref, gone_ref, degrees_ref,
    image_sem, load_sem, part_send, part_recv, lat_send, lat_recv, deg_send, deg_recv,
):
    tm, lat = lax.axis_index("tm"), lax.axis_index("lat")
    blocks, time_count, lat_count, width = parts_ref.shape
    frame_count, _, nlon = image_ref.shape[1:]
    half = nlon // 2
    pairs = seed_ref.shape[3]
    south = lat >= lat_count // 2
    north_count = lat_count // 2

    def wrap(value, count):
        return jnp.where(value >= count, value - count, value)

    def time_peer(d):
        return wrap(tm + d, time_count)

    def lat_peer(d):
        return wrap(lat + d, lat_count)

    loads = [
        pltpu.make_async_copy(own_hbm, own_ref, load_sem.at[0]),
        pltpu.make_async_copy(seed_hbm, seed_ref, load_sem.at[1]),
        pltpu.make_async_copy(time_hbm.at[tm], time_ref, load_sem.at[2]),
        pltpu.make_async_copy(grid_hbm, grid_ref, load_sem.at[3]),
    ]
    for load in loads:
        load.start()

    def image_copy(g):
        at = pl.multiple_of(jnp.where(south, blocks - 1 - g, g) * ROWS, ROWS)
        return pltpu.make_async_copy(
            frames_ref.at[:, pl.ds(at, ROWS), :], image_ref.at[g], image_sem.at[g]
        )

    image_copy(0).start()

    barrier = pltpu.get_barrier_semaphore()

    def greet_time(d):
        pl.semaphore_signal(barrier, inc=1, device_id={"tm": time_peer(d)}, device_id_type=MESH)

    def greet_lat(d):
        pl.semaphore_signal(barrier, inc=1, device_id={"lat": lat_peer(d)}, device_id_type=MESH)

    run(1, time_count, greet_time)
    run(1, lat_count, greet_lat)

    ring = time_count // 2
    row = jnp.where(tm >= ring, 1, 0)
    column = tm - row * ring

    def part_peer(d):
        dx, dy = ORDER[d - 1]
        return (1 - row if dy else row) * ring + wrap(column + dx, ring)

    def part_copy(g, d):
        peer = part_peer(d)
        return pltpu.make_async_remote_copy(
            src_ref=sent_ref.at[g, peer], dst_ref=parts_ref.at[g, tm],
            send_sem=part_send.at[g, d], recv_sem=part_recv.at[g, tm],
            device_id={"tm": peer}, device_id_type=MESH,
        )

    def part_arrival(g, d):
        peer = part_peer(d)
        return pltpu.make_async_remote_copy(
            src_ref=sent_ref.at[g, peer], dst_ref=parts_ref.at[g, peer],
            send_sem=part_send.at[g, d], recv_sem=part_recv.at[g, peer],
            device_id={"tm": peer}, device_id_type=MESH,
        )

    def band_copy(h, d):
        peer = lat_peer(d)
        return pltpu.make_async_remote_copy(
            src_ref=away_ref.at[h, peer], dst_ref=band_ref.at[h, lat],
            send_sem=lat_send.at[h, d], recv_sem=lat_recv.at[h, lat],
            device_id={"lat": peer}, device_id_type=MESH,
        )

    def band_arrival(h, d):
        peer = lat_peer(d)
        return pltpu.make_async_remote_copy(
            src_ref=away_ref.at[h, peer], dst_ref=band_ref.at[h, peer],
            send_sem=lat_send.at[h, d], recv_sem=lat_recv.at[h, peer],
            device_id={"lat": peer}, device_id_type=MESH,
        )

    def degree_copy(peer):
        return pltpu.make_async_remote_copy(
            src_ref=gone_ref.at[peer], dst_ref=degrees_ref.at[tm],
            send_sem=deg_send.at[peer], recv_sem=deg_recv.at[tm],
            device_id={"tm": peer}, device_id_type=MESH,
        )

    def degree_arrival(d):
        peer = time_peer(d)
        return pltpu.make_async_remote_copy(
            src_ref=gone_ref.at[peer], dst_ref=degrees_ref.at[peer],
            send_sem=deg_send.at[peer], recv_sem=deg_recv.at[peer],
            device_id={"tm": peer}, device_id_type=MESH,
        )

    for load in loads:
        load.wait()
    longitude_table(seed_ref, tab_ref)
    time_product_table(time_ref, wk_ref, south)
    slot_table(own_ref, ot_ref, oh_ref, time_count, lat_count)
    pl.semaphore_wait(barrier, time_count + lat_count - 2)

    def block(g):
        image_copy(g).wait()

        @pl.when(g + 1 < blocks)
        def _():
            image_copy(g + 1).start()

        image = image_ref[g].reshape(frame_count * ROWS, nlon)
        first, second = image[:, :half], image[:, half:]
        bands = []
        for parity in range(2):
            folded = first + second if parity == 0 else first - second
            coef = jnp.dot(folded, tab_ref[parity], preferred_element_type=F32).astype(BF16)
            part = jnp.dot(wk_ref[0], coef[:, :pairs], preferred_element_type=F32)
            part = part + jnp.dot(wk_ref[1], coef[:, pairs:], preferred_element_type=F32)
            bands.append(part.astype(BF16))
        both = jnp.concatenate(bands, axis=1)
        moved = lax.dot_general(
            oh_ref[...], both, (((1,), (1,)), ((), ())), preferred_element_type=F32
        ).astype(BF16)
        for slot in range(2):
            sent_ref[g, :, :, slot * width // 2 : (slot + 1) * width // 2] = moved[
                slot * pairs : (slot + 1) * pairs
            ].reshape(time_count, lat_count, width // 2)
        run(1, time_count, lambda d: part_copy(g, d).start())

    lax.fori_loop(0, blocks, lambda g, carry: (block(g), carry)[1], 0)

    slot = lat * (2 * time_count) + tm * 2
    held = [ot_ref[pl.ds(slot + s, 1), :] for s in range(2)]
    lane = lax.broadcasted_iota(jnp.int32, (1, 128), 1)
    first_slot = lax.rem(lane // ROWS, 2) == 0
    order = jnp.where(first_slot, held[0], held[1])
    degree_factors(order, rise_ref, fall_ref)
    cosine, log_sine, weight = (
        grid_ref[i * north_count : (i + 1) * north_count] for i in range(3)
    )
    steps = grid_ref[3 * north_count : 3 * north_count + 8]
    start = diagonal(order, held, first_slot, log_sine, weight, steps)
    fill_table(order, start, cosine, rise_ref, fall_ref, stage_ref, table_ref)

    def collect(g):
        run(1, time_count, lambda d: part_arrival(g, d).wait_recv())
        total = sent_ref[g, tm].astype(F32)
        for d in range(1, time_count):
            total = total + parts_ref[g, part_peer(d)].astype(F32)
        total_ref[g] = total

    def send_half(h):
        held_blocks = range(h * blocks // 2, (h + 1) * blocks // 2)
        for g in held_blocks:
            collect(g)
        for low in range(F):
            pieces = [
                total_ref[g, :, base + ef * ROWS : base + (ef + 1) * ROWS]
                for ef in (low, low + F)
                for g in held_blocks
                for base in (0, width // 2)
            ]
            sum_ref[pl.ds(low, lat_count, stride=F), :] = jnp.concatenate(pieces, axis=1)
        away_ref[h] = sum_ref[...].astype(BF16).reshape(away_ref.shape[1:])
        run(1, lat_count, lambda d: band_copy(h, d).start())
        band_ref[h, lat] = away_ref[h, lat]

    for h in range(2):
        send_half(h)

    lanes = lax.broadcasted_iota(jnp.int32, (F, 128), 1)
    mine = lax.rem(lanes // ROWS, 2) == 0

    def receive_half(h):
        run(1, lat_count, lambda d: band_arrival(h, d).wait_recv())
        for pair in range(north_count // 2):
            north = [band_ref[h, 2 * pair + k].astype(F32) for k in range(2)]
            mirror = [band_ref[h, lat_count - 1 - 2 * pair - k].astype(F32) for k in range(2)]
            at = slice((h * north_count // 2 + pair) * 128, (h * north_count // 2 + pair + 1) * 128)
            for sign in range(2):
                tiles = [n - m if sign else n + m for n, m in zip(north, mirror)]
                parts = [
                    jnp.concatenate([tile[:, k * 64 : (k + 1) * 64] for tile in tiles], axis=1)
                    for k in range(2)
                ]
                whole = jnp.concatenate(parts, axis=0)
                both_mine = jnp.concatenate([mine, mine], axis=0)
                base = sign * 4 * F
                both_ref[base : base + 2 * F, at] = jnp.where(both_mine, whole, 0.0).astype(BF16)
                both_ref[base + 2 * F : base + 4 * F, at] = jnp.where(
                    both_mine, 0.0, whole
                ).astype(BF16)

    depth = both_ref.shape[1] // 2

    def half_product(h, base):
        return lax.dot_general(
            both_ref[:, h * depth : (h + 1) * depth],
            table_ref[pl.ds(base, 256), h * depth : (h + 1) * depth],
            (((1,), (1,)), ((), ())),
            preferred_element_type=F32,
        )

    receive_half(0)
    for base in range(0, L, 256):
        acc_ref[base // 256] = half_product(0, base)
    receive_half(1)

    def product(d):
        pair = wrap(tm // 2 + d, time_count // 2)
        base = pl.multiple_of(pair * 256, 256)
        piece = acc_ref[pair] + half_product(1, base)
        level = (base + lax.broadcasted_iota(jnp.int32, (2 * F, 256), 1)).astype(F32)
        for s in range(2):
            offset = level + held[s][:, :1]
            odd = offset - 2.0 * jnp.floor(offset * 0.5)
            at = slice(2 * F * s, 2 * F * (s + 1))
            even_part, odd_part = piece[at], piece[4 * F + 2 * F * s : 4 * F + 2 * F * (s + 1)]
            chosen = jnp.where(odd == 0.0, even_part, odd_part)
            for k in range(2):
                gone_ref[2 * pair + k, at] = chosen[:, k * 128 : (k + 1) * 128]
        for k in range(2):
            peer = 2 * pair + k

            @pl.when(peer != tm)
            def _():
                degree_copy(peer).start()

    for d in range(1, time_count // 2 + 1):
        product(d)
    degrees_ref[tm] = gone_ref[tm]
    run(1, time_count, lambda d: degree_arrival(d).wait_recv())
    for peer in range(time_count):
        for s in range(2):
            for e in range(2):
                at = (2 * s + e) * F
                out_ref[e, 2 * peer + s] = degrees_ref[peer, at : at + F, :]
    run(0, blocks, lambda g: run(1, time_count, lambda d: part_copy(g, d).wait_send()))
    for h in range(2):
        run(1, lat_count, lambda d: band_copy(h, d).wait_send())
    run(1, time_count, lambda d: degree_copy(time_peer(d)).wait_send())


def shards(frames, owner_map):
    lat_count = lax.axis_size("lat")
    time_count = lax.axis_size("tm")
    frame_count, lat_rows, nlon = frames.shape
    orders = owner_map.shape[0]
    blocks = lat_rows // ROWS
    size = frame_count * ROWS
    width = 2 * 2 * F * ROWS
    seeds = longitude_seeds(nlon, orders)
    times = time_tables(time_count, frame_count)
    grids = latitude_constants(lat_count * lat_rows, lat_rows)
    hbm = pl.BlockSpec(memory_space=pltpu.HBM)
    dma = pltpu.SemaphoreType.DMA
    return pl.pallas_call(
        kernel,
        out_shape=jax.ShapeDtypeStruct((2, 2 * time_count, F, L // time_count), F32),
        in_specs=[hbm] * 5,
        out_specs=pl.BlockSpec(memory_space=pltpu.VMEM),
        scratch_shapes=[
            pltpu.VMEM((blocks, frame_count, ROWS, nlon), BF16),
            pltpu.VMEM((1, orders), jnp.int32),
            pltpu.VMEM(seeds.shape, F32),
            pltpu.VMEM(times.shape[1:], F32),
            pltpu.VMEM(grids.shape, F32),
            pltpu.VMEM((2, nlon // 2, orders), BF16),
            pltpu.VMEM((2, size, size), BF16),
            pltpu.VMEM((orders, 128), F32),
            pltpu.VMEM((orders, orders), BF16),
            pltpu.VMEM((blocks, time_count, lat_count, width), BF16),
            pltpu.VMEM((L, 128), F32),
            pltpu.VMEM((L, 128), F32),
            pltpu.VMEM((lat_count * 8, 128), F32),
            pltpu.VMEM((L, lat_count * 64), BF16),
            pltpu.VMEM((8 * F, lat_count * 64), BF16),
            pltpu.VMEM((L // 256, 8 * F, 256), F32),
            pltpu.VMEM((blocks, time_count, lat_count, width), BF16),
            pltpu.VMEM((blocks, lat_count, width), F32),
            pltpu.VMEM((lat_count * F, 128), F32),
            pltpu.VMEM((2, lat_count, F, 128), BF16),
            pltpu.VMEM((2, lat_count, F, 128), BF16),
            pltpu.VMEM((time_count, 4 * F, 128), F32),
            pltpu.VMEM((time_count, 4 * F, 128), F32),
            dma((blocks,)), dma((4,)),
            dma((blocks, time_count)), dma((blocks, time_count)),
            dma((2, lat_count)), dma((2, lat_count)),
            dma((time_count,)), dma((time_count,)),
        ],
        compiler_params=pltpu.CompilerParams(
            vmem_limit_bytes=56 << 20, collective_id=0, has_side_effects=True
        ),
        name="spectrum",
    )(
        frames, owner_map.reshape(1, orders),
        jnp.asarray(seeds), jnp.asarray(times), jnp.asarray(grids),
    )


def solution(mesh):
    return jax.shard_map(
        shards,
        mesh=mesh,
        in_specs=(P("tm", "lat", None), P()),
        out_specs=P(None, "lat", None, "tm"),
        check_vma=False,
    )
```

```python
from functools import partial
import math

import jax
import jax.numpy as jnp
from jax import lax
from jax.experimental import pallas as pl
from jax.experimental.pallas import tpu as pltpu
from jax.sharding import PartitionSpec as P
import numpy as np

L = 1024
F = 8
BF16 = jnp.bfloat16
MESH = pl.DeviceIdType.MESH
F32 = jnp.float32


ROWS = 16
ORDER = ((2, 1), (1, 1), (3, 1), (0, 1), (2, 0), (1, 0), (3, 0))
FINE = 64


def longitude_seeds(nlon, orders):
    count = nlon // 2 // FINE
    seeds = []
    for parity in range(2):
        order = np.arange(parity, orders, 2, dtype=np.int64)[None, :]
        points = np.concatenate([np.arange(count) * FINE, np.arange(FINE)])[:, None]
        angles = (points * order % nlon) * (2.0 * math.pi / nlon)
        scale = np.where(np.arange(count + FINE)[:, None] < count, math.sqrt(2.0 / nlon), 1.0)
        seeds.append(np.stack([np.cos(angles) * scale, np.sin(angles) * scale]))
    return np.stack(seeds).astype(np.float32)


def time_tables(parts, frames):
    total = parts * frames
    times = np.arange(total, dtype=np.int64)[None, :]
    frequency = (total // 8 + np.arange(F, dtype=np.int64))[:, None]
    angles = (frequency * times % total) * (2.0 * math.pi / total)
    cos_part = np.cos(angles) / math.sqrt(total)
    sin_part = np.sin(angles) / math.sqrt(total)
    real = np.concatenate([cos_part, -sin_part], axis=0)
    imag = np.concatenate([sin_part, cos_part], axis=0)
    table = np.stack([real, imag]).reshape(2, 2 * F, parts, frames).transpose(2, 0, 1, 3)
    return np.repeat(table, ROWS, axis=3).astype(np.float32)


def latitude_constants(nlat, lat_rows):
    colatitude = (np.arange(nlat // 2) + 0.5) * (math.pi / nlat)
    sine = np.sin(colatitude)
    weight = sine * (math.pi / nlat) * math.sqrt(nlat)

    def lay(values):
        values = values.reshape(-1, 2, 2, lat_rows // ROWS // 2, 1, ROWS)
        values = np.repeat(values.transpose(2, 0, 1, 3, 4, 5), 2, axis=4)
        return values.reshape(-1, 2 * lat_rows)

    steps = np.log1p(0.5 / np.arange(1, 1025)).reshape(8, 128)
    parts = [lay(np.cos(colatitude)), lay(np.log(sine)), lay(weight), steps]
    return np.concatenate(parts).astype(np.float32)


def longitude_table(seed_ref, tab_ref):
    pairs = seed_ref.shape[3]
    count = seed_ref.shape[2] - FINE
    for parity in range(2):

        def body(i, carry):
            cos_row = seed_ref[parity, 0, pl.ds(i, 1), :]
            sin_row = seed_ref[parity, 1, pl.ds(i, 1), :]
            near_cos, near_sin = seed_ref[parity, 0, count:], seed_ref[parity, 1, count:]
            at = pl.ds(pl.multiple_of(i * FINE, FINE), FINE)
            tab_ref[parity, at, :pairs] = (cos_row * near_cos - sin_row * near_sin).astype(BF16)
            tab_ref[parity, at, pairs:] = (-sin_row * near_cos - cos_row * near_sin).astype(BF16)
            return carry

        lax.fori_loop(0, count, body, 0)


def time_product_table(time_ref, wk_ref, flip):
    size = wk_ref.shape[1]
    row = lax.broadcasted_iota(jnp.int32, (ROWS, size), 0)
    lane = lax.rem(lax.broadcasted_iota(jnp.int32, (ROWS, size), 1), ROWS)
    same = row == jnp.where(flip, ROWS - 1 - lane, lane)
    for c in range(2):
        for ef in range(2 * F):
            line = jnp.broadcast_to(time_ref[c, ef : ef + 1, :], (ROWS, size))
            wk_ref[c, ef * ROWS : (ef + 1) * ROWS, :] = jnp.where(same, line, 0.0).astype(BF16)


def slot_table(own_ref, ot_ref, oh_ref, time_count, lat_count):
    orders = own_ref.shape[1]
    pairs = orders // 2
    wide = jnp.broadcast_to(own_ref[...].astype(F32), (128, orders))
    for block in range(orders // 128):
        ot_ref[block * 128 : (block + 1) * 128, :] = wide[:, block * 128 : (block + 1) * 128].T
    lane = lax.broadcasted_iota(jnp.int32, (lat_count, orders), 1)
    order = jnp.where(lane < pairs, 2 * lane, 2 * (lane - pairs) + 1).astype(F32)
    for slot in range(2):
        for peer in range(time_count):
            held = ot_ref[pl.ds(2 * peer + slot, lat_count, stride=2 * time_count), :]
            held = jnp.concatenate([held] * (orders // 128), axis=1)
            at = (slot * time_count + peer) * lat_count
            oh_ref[at : at + lat_count, :] = jnp.where(held == order, 1.0, 0.0).astype(BF16)


def degree_factors(order, rise_ref, fall_ref):
    block = 64

    def body(i, carry):
        at = pl.multiple_of(i * block, block)
        level = (at + lax.broadcasted_iota(jnp.int32, (block, 128), 0)).astype(F32)
        level_sq = level * level
        order_sq = order * order
        lower = level - 1.0
        rising = jnp.sqrt(
            jnp.maximum(4.0 * level_sq - 1.0, 0.0) / jnp.maximum(level_sq - order_sq, 1.0)
        )
        falling = jnp.sqrt(
            jnp.maximum(lower * lower - order_sq, 0.0)
            / jnp.maximum(4.0 * lower * lower - 1.0, 1.0)
        )
        rise_ref[pl.ds(at, block), :] = rising
        fall_ref[pl.ds(at, block), :] = rising * falling
        return carry

    lax.fori_loop(0, L // block, body, 0)


def diagonal(order, held, first, log_sine, weight, steps):
    step = (
        128 * lax.broadcasted_iota(jnp.int32, (8, 128), 0)
        + lax.broadcasted_iota(jnp.int32, (8, 128), 1)
        + 1
    ).astype(F32)
    sums = [jnp.sum(jnp.where(step <= m, steps, 0.0), axis=(0, 1), keepdims=True) for m in held]
    growth = jnp.where(first, sums[0], sums[1])
    lognorm = 0.5 * math.log(0.5) + 0.5 * growth + order * log_sine
    start = jnp.where(lognorm >= -60.0, jnp.exp(jnp.maximum(lognorm, -60.0)), 0.0)
    return start * weight


def fill_table(order, start, cosine, rise_ref, fall_ref, stage_ref, table_ref):
    groups = start.shape[0] // 8
    span = 16
    wide_order = jnp.broadcast_to(order, (8, 128))

    def body(i, carry):
        base = pl.multiple_of(i * span, span)
        newer, older = list(carry[0]), list(carry[1])
        for k in range(span):
            rise = jnp.broadcast_to(rise_ref[pl.ds(base + k, 1), :], (8, 128))
            fall = jnp.broadcast_to(fall_ref[pl.ds(base + k, 1), :], (8, 128))
            first = wide_order == (base + k).astype(F32)
            for g in range(groups):
                at = slice(8 * g, 8 * g + 8)
                now = (rise * cosine[at]) * newer[g] - fall * older[g]
                now = jnp.where(first, start[at], now)
                newer[g], older[g] = now, newer[g]
                stage_ref[(g * span + k) * 8 : (g * span + k) * 8 + 8, :] = now
        for g in range(groups):
            for j in range(8):
                rows = stage_ref[pl.ds(g * span * 8 + j, span, stride=8), :]
                table_ref[pl.ds(base, span), (8 * g + j) * 128 : (8 * g + j + 1) * 128] = (
                    rows.astype(BF16)
                )
        return tuple(newer), tuple(older)

    zeros = tuple(jnp.zeros((8, 128), F32) for _ in range(groups))
    lax.fori_loop(0, L // span, body, (zeros, zeros))


def run(first, last, action):
    def body(d, carry):
        action(d)
        return carry

    if last - first < 8:
        for d in range(first, last):
            action(d)
    else:
        lax.fori_loop(first, last, body, 0, unroll=True)


def kernel(
    frames_ref, own_hbm, seed_hbm, time_hbm, grid_hbm, out_ref,
    image_ref, own_ref, seed_ref, time_ref, grid_ref,
    tab_ref, wk_ref, ot_ref, oh_ref, sent_ref,
    rise_ref, fall_ref, stage_ref, table_ref, both_ref, acc_ref,
    parts_ref, total_ref, sum_ref, away_ref, band_ref, gone_ref, degrees_ref,
    image_sem, load_sem, part_send, part_recv, lat_send, lat_recv, deg_send, deg_recv,
):
    tm, lat = lax.axis_index("tm"), lax.axis_index("lat")
    blocks, time_count, lat_count, width = parts_ref.shape
    frame_count, _, nlon = image_ref.shape[1:]
    half = nlon // 2
    pairs = seed_ref.shape[3]
    south = lat >= lat_count // 2
    north_count = lat_count // 2

    def wrap(value, count):
        return jnp.where(value >= count, value - count, value)

    def time_peer(d):
        return wrap(tm + d, time_count)

    def lat_peer(d):
        return wrap(lat + d, lat_count)

    loads = [
        pltpu.make_async_copy(own_hbm, own_ref, load_sem.at[0]),
        pltpu.make_async_copy(seed_hbm, seed_ref, load_sem.at[1]),
        pltpu.make_async_copy(time_hbm.at[tm], time_ref, load_sem.at[2]),
        pltpu.make_async_copy(grid_hbm, grid_ref, load_sem.at[3]),
    ]
    for load in loads:
        load.start()

    def image_copy(g):
        at = pl.multiple_of(jnp.where(south, blocks - 1 - g, g) * ROWS, ROWS)
        return pltpu.make_async_copy(
            frames_ref.at[:, pl.ds(at, ROWS), :], image_ref.at[g], image_sem.at[g]
        )

    image_copy(0).start()

    barrier = pltpu.get_barrier_semaphore()

    def greet_time(d):
        pl.semaphore_signal(barrier, inc=1, device_id={"tm": time_peer(d)}, device_id_type=MESH)

    def greet_lat(d):
        pl.semaphore_signal(barrier, inc=1, device_id={"lat": lat_peer(d)}, device_id_type=MESH)

    run(1, time_count, greet_time)
    run(1, lat_count, greet_lat)

    ring = time_count // 2
    row = jnp.where(tm >= ring, 1, 0)
    column = tm - row * ring

    def part_peer(d):
        dx, dy = ORDER[d - 1]
        return (1 - row if dy else row) * ring + wrap(column + dx, ring)

    def part_copy(g, d):
        peer = part_peer(d)
        return pltpu.make_async_remote_copy(
            src_ref=sent_ref.at[g, peer], dst_ref=parts_ref.at[g, tm],
            send_sem=part_send.at[g, d], recv_sem=part_recv.at[g, tm],
            device_id={"tm": peer}, device_id_type=MESH,
        )

    def part_arrival(g, d):
        peer = part_peer(d)
        return pltpu.make_async_remote_copy(
            src_ref=sent_ref.at[g, peer], dst_ref=parts_ref.at[g, peer],
            send_sem=part_send.at[g, d], recv_sem=part_recv.at[g, peer],
            device_id={"tm": peer}, device_id_type=MESH,
        )

    def band_copy(h, d):
        peer = lat_peer(d)
        return pltpu.make_async_remote_copy(
            src_ref=away_ref.at[h, peer], dst_ref=band_ref.at[h, lat],
            send_sem=lat_send.at[h, d], recv_sem=lat_recv.at[h, lat],
            device_id={"lat": peer}, device_id_type=MESH,
        )

    def band_arrival(h, d):
        peer = lat_peer(d)
        return pltpu.make_async_remote_copy(
            src_ref=away_ref.at[h, peer], dst_ref=band_ref.at[h, peer],
            send_sem=lat_send.at[h, d], recv_sem=lat_recv.at[h, peer],
            device_id={"lat": peer}, device_id_type=MESH,
        )

    def degree_copy(peer):
        return pltpu.make_async_remote_copy(
            src_ref=gone_ref.at[peer], dst_ref=degrees_ref.at[tm],
            send_sem=deg_send.at[peer], recv_sem=deg_recv.at[tm],
            device_id={"tm": peer}, device_id_type=MESH,
        )

    def degree_arrival(d):
        peer = time_peer(d)
        return pltpu.make_async_remote_copy(
            src_ref=gone_ref.at[peer], dst_ref=degrees_ref.at[peer],
            send_sem=deg_send.at[peer], recv_sem=deg_recv.at[peer],
            device_id={"tm": peer}, device_id_type=MESH,
        )

    for load in loads:
        load.wait()
    longitude_table(seed_ref, tab_ref)
    time_product_table(time_ref, wk_ref, south)
    slot_table(own_ref, ot_ref, oh_ref, time_count, lat_count)
    pl.semaphore_wait(barrier, time_count + lat_count - 2)

    def block(g):
        image_copy(g).wait()

        @pl.when(g + 1 < blocks)
        def _():
            image_copy(g + 1).start()

        image = image_ref[g].reshape(frame_count * ROWS, nlon)
        first, second = image[:, :half], image[:, half:]
        bands = []
        for parity in range(2):
            folded = first + second if parity == 0 else first - second
            coef = jnp.dot(folded, tab_ref[parity], preferred_element_type=F32).astype(BF16)
            part = jnp.dot(wk_ref[0], coef[:, :pairs], preferred_element_type=F32)
            part = part + jnp.dot(wk_ref[1], coef[:, pairs:], preferred_element_type=F32)
            bands.append(part.astype(BF16))
        both = jnp.concatenate(bands, axis=1)
        moved = lax.dot_general(
            oh_ref[...], both, (((1,), (1,)), ((), ())), preferred_element_type=F32
        ).astype(BF16)
        for slot in range(2):
            sent_ref[g, :, :, slot * width // 2 : (slot + 1) * width // 2] = moved[
                slot * pairs : (slot + 1) * pairs
            ].reshape(time_count, lat_count, width // 2)
        run(1, time_count, lambda d: part_copy(g, d).start())

    lax.fori_loop(0, blocks, lambda g, carry: (block(g), carry)[1], 0)

    slot = lat * (2 * time_count) + tm * 2
    held = [ot_ref[pl.ds(slot + s, 1), :] for s in range(2)]
    lane = lax.broadcasted_iota(jnp.int32, (1, 128), 1)
    first_slot = lax.rem(lane // ROWS, 2) == 0
    order = jnp.where(first_slot, held[0], held[1])
    degree_factors(order, rise_ref, fall_ref)
    cosine, log_sine, weight = (
        grid_ref[i * north_count : (i + 1) * north_count] for i in range(3)
    )
    steps = grid_ref[3 * north_count : 3 * north_count + 8]
    start = diagonal(order, held, first_slot, log_sine, weight, steps)
    fill_table(order, start, cosine, rise_ref, fall_ref, stage_ref, table_ref)

    def collect(g):
        run(1, time_count, lambda d: part_arrival(g, d).wait_recv())
        total = sent_ref[g, tm].astype(F32)
        for d in range(1, time_count):
            total = total + parts_ref[g, part_peer(d)].astype(F32)
        total_ref[g] = total

    def send_half(h):
        held_blocks = range(h * blocks // 2, (h + 1) * blocks // 2)
        for g in held_blocks:
            collect(g)
        for low in range(F):
            pieces = [
                total_ref[g, :, base + ef * ROWS : base + (ef + 1) * ROWS]
                for ef in (low, low + F)
                for g in held_blocks
                for base in (0, width // 2)
            ]
            sum_ref[pl.ds(low, lat_count, stride=F), :] = jnp.concatenate(pieces, axis=1)
        away_ref[h] = sum_ref[...].astype(BF16).reshape(away_ref.shape[1:])
        span = lat_count // 4
        for d in sorted(range(1, lat_count), key=lambda d: -min(d // 2 % span, -(d // 2) % span)):
            band_copy(h, d).start()
        band_ref[h, lat] = away_ref[h, lat]

    for h in range(2):
        send_half(h)

    lanes = lax.broadcasted_iota(jnp.int32, (F, 128), 1)
    mine = lax.rem(lanes // ROWS, 2) == 0

    def receive_half(h):
        run(1, lat_count, lambda d: band_arrival(h, d).wait_recv())
        for pair in range(north_count // 2):
            north = [band_ref[h, 2 * pair + k].astype(F32) for k in range(2)]
            mirror = [band_ref[h, lat_count - 1 - 2 * pair - k].astype(F32) for k in range(2)]
            at = slice((h * north_count // 2 + pair) * 128, (h * north_count // 2 + pair + 1) * 128)
            for sign in range(2):
                tiles = [n - m if sign else n + m for n, m in zip(north, mirror)]
                parts = [
                    jnp.concatenate([tile[:, k * 64 : (k + 1) * 64] for tile in tiles], axis=1)
                    for k in range(2)
                ]
                whole = jnp.concatenate(parts, axis=0)
                both_mine = jnp.concatenate([mine, mine], axis=0)
                base = sign * 4 * F
                both_ref[base : base + 2 * F, at] = jnp.where(both_mine, whole, 0.0).astype(BF16)
                both_ref[base + 2 * F : base + 4 * F, at] = jnp.where(
                    both_mine, 0.0, whole
                ).astype(BF16)

    depth = both_ref.shape[1] // 2

    def half_product(h, base):
        return lax.dot_general(
            both_ref[:, h * depth : (h + 1) * depth],
            table_ref[pl.ds(base, 256), h * depth : (h + 1) * depth],
            (((1,), (1,)), ((), ())),
            preferred_element_type=F32,
        )

    receive_half(0)
    for base in range(0, L, 256):
        acc_ref[base // 256] = half_product(0, base)
    receive_half(1)

    def product(d):
        pair = wrap(tm // 2 + d, time_count // 2)
        base = pl.multiple_of(pair * 256, 256)
        piece = acc_ref[pair] + half_product(1, base)
        level = (base + lax.broadcasted_iota(jnp.int32, (2 * F, 256), 1)).astype(F32)
        for s in range(2):
            offset = level + held[s][:, :1]
            odd = offset - 2.0 * jnp.floor(offset * 0.5)
            at = slice(2 * F * s, 2 * F * (s + 1))
            even_part, odd_part = piece[at], piece[4 * F + 2 * F * s : 4 * F + 2 * F * (s + 1)]
            chosen = jnp.where(odd == 0.0, even_part, odd_part)
            for k in range(2):
                gone_ref[2 * pair + k, at] = chosen[:, k * 128 : (k + 1) * 128]
        for k in range(2):
            peer = 2 * pair + k

            @pl.when(peer != tm)
            def _():
                degree_copy(peer).start()

    for d in range(1, time_count // 2 + 1):
        product(d)
    degrees_ref[tm] = gone_ref[tm]
    run(1, time_count, lambda d: degree_arrival(d).wait_recv())
    for peer in range(time_count):
        for s in range(2):
            for e in range(2):
                at = (2 * s + e) * F
                out_ref[e, 2 * peer + s] = degrees_ref[peer, at : at + F, :]
    run(0, blocks, lambda g: run(1, time_count, lambda d: part_copy(g, d).wait_send()))
    for h in range(2):
        run(1, lat_count, lambda d: band_copy(h, d).wait_send())
    run(1, time_count, lambda d: degree_copy(time_peer(d)).wait_send())


def shards(frames, owner_map):
    lat_count = lax.axis_size("lat")
    time_count = lax.axis_size("tm")
    frame_count, lat_rows, nlon = frames.shape
    orders = owner_map.shape[0]
    blocks = lat_rows // ROWS
    size = frame_count * ROWS
    width = 2 * 2 * F * ROWS
    seeds = longitude_seeds(nlon, orders)
    times = time_tables(time_count, frame_count)
    grids = latitude_constants(lat_count * lat_rows, lat_rows)
    hbm = pl.BlockSpec(memory_space=pltpu.HBM)
    dma = pltpu.SemaphoreType.DMA
    return pl.pallas_call(
        kernel,
        out_shape=jax.ShapeDtypeStruct((2, 2 * time_count, F, L // time_count), F32),
        in_specs=[hbm] * 5,
        out_specs=pl.BlockSpec(memory_space=pltpu.VMEM),
        scratch_shapes=[
            pltpu.VMEM((blocks, frame_count, ROWS, nlon), BF16),
            pltpu.VMEM((1, orders), jnp.int32),
            pltpu.VMEM(seeds.shape, F32),
            pltpu.VMEM(times.shape[1:], F32),
            pltpu.VMEM(grids.shape, F32),
            pltpu.VMEM((2, nlon // 2, orders), BF16),
            pltpu.VMEM((2, size, size), BF16),
            pltpu.VMEM((orders, 128), F32),
            pltpu.VMEM((orders, orders), BF16),
            pltpu.VMEM((blocks, time_count, lat_count, width), BF16),
            pltpu.VMEM((L, 128), F32),
            pltpu.VMEM((L, 128), F32),
            pltpu.VMEM((lat_count * 8, 128), F32),
            pltpu.VMEM((L, lat_count * 64), BF16),
            pltpu.VMEM((8 * F, lat_count * 64), BF16),
            pltpu.VMEM((L // 256, 8 * F, 256), F32),
            pltpu.VMEM((blocks, time_count, lat_count, width), BF16),
            pltpu.VMEM((blocks, lat_count, width), F32),
            pltpu.VMEM((lat_count * F, 128), F32),
            pltpu.VMEM((2, lat_count, F, 128), BF16),
            pltpu.VMEM((2, lat_count, F, 128), BF16),
            pltpu.VMEM((time_count, 4 * F, 128), F32),
            pltpu.VMEM((time_count, 4 * F, 128), F32),
            dma((blocks,)), dma((4,)),
            dma((blocks, time_count)), dma((blocks, time_count)),
            dma((2, lat_count)), dma((2, lat_count)),
            dma((time_count,)), dma((time_count,)),
        ],
        compiler_params=pltpu.CompilerParams(
            vmem_limit_bytes=56 << 20, collective_id=0, has_side_effects=True
        ),
        name="spectrum",
    )(
        frames, owner_map.reshape(1, orders),
        jnp.asarray(seeds), jnp.asarray(times), jnp.asarray(grids),
    )


def solution(mesh):
    return jax.shard_map(
        shards,
        mesh=mesh,
        in_specs=(P("tm", "lat", None), P()),
        out_specs=P(None, "lat", None, "tm"),
        check_vma=False,
    )
```
